128 devices in a mesh: order: 8 (over x_lo, y), chan: 16 (over x_hi, z, core).
Axes of the slice: x: 4 (x_hi: 2, x_lo: 2; x = x_hi * 2 + x_lo), y: 4, z: 4, core: 2. Of those that a mesh axis runs over, the one named last changes fastest.
Arguments:
- grad_out: bfloat16 [3, 256, 720, 1440], P(None, 'chan', 'order'), may hold values from -6 to 6
- legendre: bfloat16 [96, 720, 768], P('order', 'chan'), as said below
- filter_re: float32 [256, 720], P('chan'), may hold values from -6 to 6
- filter_im: float32 [256, 720], P('chan'), may hold values from -6 to 6
- quad_weight: float32 [720], P('order'), may hold values from 0.5 to 2
- pair_order: int32 [96], replicated, may hold values from 0 to 359, as said below
Outputs:
- grad_in: bfloat16 [3, 256, 720, 1440], P(None, 'chan', 'order')
The draws below stay inside these ranges and needn't reach their ends.
Inputs may be any that keep to these rules, and one draw needn't show every extreme that they name: `pair_order`: the values are distinct. Slot j belongs to index j // 12 of order. `legendre`: entries in rows r > 720 of the last dimension are zero.
All inputs are finite; a program needn't handle non-finite values.
Results may differ from the reference program's by a relative error of at most 0.0072.
Values may be sent and summed in bfloat16 or wider, within the bound.
No kernel may reach another device: no remote copies, remote signals or barrier semaphores. Data moves between devices by JAX's collectives and lax.ppermute only.
A program may use at most 128 MiB of HBM per device.

```python
import math
import jax
import jax.numpy as jnp
from jax import lax

C = 256
NLAT = 720
NLON = 1440
M = 720
SAMPLES = 3
PAIRS = 96
LROWS = 768


def draw_pair_order(key, part):
    return jax.random.permutation(key, M // 2)[:PAIRS].astype(jnp.int32)


def draw_legendre(key, part):
    values = jax.random.normal(key, (PAIRS, NLAT, LROWS), jnp.float32)
    row_ids = jnp.arange(LROWS, dtype=jnp.int32)
    live = (row_ids <= M).astype(jnp.float32)
    return (values * live[None, None, :] * NLAT ** (-0.5)).astype(jnp.bfloat16)


def steps_of(rng, dims, cuts, smallest, top_value):
    level, own = 1.0, jax.random.fold_in(rng, 6)
    for position, blocks in cuts:
        heights = jnp.exp(jax.random.uniform(jax.random.fold_in(own, position), (blocks,), jnp.float32, smallest / len(cuts), top_value / len(cuts)))
        level = level * jnp.repeat(heights, dims[position] // blocks).reshape([-1 if axis == position else 1 for axis in range(len(dims))])
    return level


def normal_values(rng, shape, scale, reach, pieces=(), held_as=jnp.bfloat16):
    factor_of = steps_of(rng, shape, pieces, -0.22, 0.18) if pieces else 1.0
    entries = jax.random.normal(rng, shape, jnp.float32) * scale * factor_of
    return jnp.minimum(jnp.maximum(entries, -reach), reach).astype(held_as)


def setup_inputs(seed: int = 0) -> dict:
    seeds = jax.random.split(jax.random.key(seed), 7)
    return {
        "grad_out": normal_values(seeds[0], (SAMPLES, C, NLAT, NLON), 1.0, 6.0, ((1, 16), (2, 8))),
        "legendre": draw_legendre(jax.random.fold_in(seeds[6], 71), 0),
        "filter_re": normal_values(seeds[2], (C, M), 1.0, 6.0, ((0, 16),), jnp.float32),
        "filter_im": normal_values(seeds[3], (C, M), 1.0, 6.0, ((0, 16),), jnp.float32),
        "quad_weight": jnp.clip(jnp.exp(math.log(2.0) - 1.3862944 * jax.random.uniform(seeds[4], (NLAT,), jnp.float32) ** steps_of(seeds[4], (NLAT,), ((0, 8),), -0.2, 0.2)), 0.5, 2.0),
        "pair_order": draw_pair_order(jax.random.fold_in(seeds[6], 71), 0),
    }


def basis_tables(pair_order):
    low_order = pair_order.astype(jnp.int32)
    high_order = M - 1 - low_order
    orders = jnp.stack([low_order, low_order, high_order, high_order], axis=1).reshape(-1)
    columns = orders.shape[0]
    parity = jnp.arange(columns, dtype=jnp.int32) % 2
    longitude = jnp.arange(NLON, dtype=jnp.int32)
    phases = (longitude[:, None] * orders[None, :]) % NLON
    angles = phases.astype(jnp.float32) * (2.0 * math.pi / NLON)
    fourier = jnp.where(parity[None, :] == 0, jnp.cos(angles), -jnp.sin(angles))
    factor = jnp.where(orders == 0, 1.0, 2.0).astype(jnp.float32)
    forward = (fourier * factor[None, :]).astype(jnp.bfloat16)
    inverse = fourier.T.astype(jnp.bfloat16)
    return forward, inverse


def spectral_masks(low_order):
    row_ids = jnp.arange(LROWS, dtype=jnp.int32)
    below = row_ids[None, :] < (M - low_order)[:, None]
    degree = jnp.where(below, low_order[:, None] + row_ids[None, :], row_ids[None, :] - 1)
    return below, jnp.clip(degree, 0, M - 1).astype(jnp.int32)


def apply_filter(spectrum, low_order, filter_re, filter_im):
    below, degree = spectral_masks(low_order)
    channels = filter_re.shape[0]
    pairs, rows = degree.shape
    gain_re = jnp.take(filter_re, degree.reshape(-1), axis=1).reshape(channels, pairs, rows)
    gain_im = jnp.take(filter_im, degree.reshape(-1), axis=1).reshape(channels, pairs, rows)
    gain_re = jnp.transpose(gain_re, (1, 2, 0))[:, :, None, :]
    gain_im = jnp.transpose(gain_im, (1, 2, 0))[:, :, None, :]
    inside = below[:, :, None, None]
    former = jnp.where(inside, spectrum[..., 0], spectrum[..., 2])
    latter = jnp.where(inside, spectrum[..., 1], spectrum[..., 3])
    real_part = gain_re * former + gain_im * latter
    imag_part = gain_re * latter - gain_im * former
    keep_mask = inside.astype(real_part.dtype)
    split = jnp.stack([real_part * keep_mask, imag_part * keep_mask,
                       real_part * (1.0 - keep_mask), imag_part * (1.0 - keep_mask)], axis=-1)
    return split.astype(jnp.bfloat16)


def reference(grad_out, legendre, filter_re, filter_im, quad_weight, pair_order):
    forward, inverse = basis_tables(pair_order)

    def transform(sample):
        flat = sample.reshape(C * NLAT, NLON)
        result = jnp.dot(flat, forward, preferred_element_type=jnp.float32).astype(jnp.bfloat16)
        return result.reshape(C, NLAT, PAIRS, 4)

    coeffs = lax.map(transform, grad_out)
    per_slot = jnp.transpose(coeffs, (3, 0, 1, 2, 4))

    def one_slot(inputs):
        table, block, lowest = inputs
        spectrum = jnp.einsum("tr,sctq->rscq", table.astype(jnp.float32), block.astype(jnp.float32))
        split = apply_filter(spectrum[None], lowest[None], filter_re, filter_im)[0]
        synth = jnp.einsum("tr,rscq->sctq", table.astype(jnp.float32), split.astype(jnp.float32))
        return synth.astype(jnp.bfloat16)

    synthesis = lax.map(one_slot, (legendre, per_slot, pair_order.astype(jnp.int32)))
    synthesis = jnp.transpose(synthesis, (1, 2, 3, 0, 4)).reshape(SAMPLES, C * NLAT, PAIRS * 4)

    def back(block):
        return jnp.dot(block, inverse, preferred_element_type=jnp.float32)

    values = lax.map(back, synthesis).reshape(SAMPLES, C, NLAT, NLON)
    scale = quad_weight * (2.0 * math.pi / NLON)
    return (values * scale[None, None, :, None]).astype(jnp.bfloat16)
```

```python
import math

import jax
import jax.numpy as jnp
from jax import lax
from jax.experimental import pallas as pl
from jax.experimental.pallas import tpu as pltpu
from jax.sharding import Mesh
from jax.sharding import PartitionSpec as P

NLON = 1440
M = 720
ROWS = 768
PAIRS = 96
SAMPLES = 3
CH = 16
LAT = 90
HALF = 45
HP = 48
DEST = 32
SLOTS = 3
GROUPS = 4
STRIPE = SLOTS * HP
LANES = 128
COLS = 4 * LANES
STEP = 16
CHUNK = 9
VMEM = 56 * 1024 * 1024

SLOT_AXES = ("x_lo", "y", "x_hi", "core")
NT = (((1,), (1,)), ((), ()))
TN = (((0,), (0,)), ((), ()))


def fill_table(low, table, coarse_cos, coarse_sin):
    orders = jnp.concatenate([low, M - 1 - low], axis=1)
    unit = 2.0 * math.pi / NLON

    def angle(count, scale):
        k = lax.broadcasted_iota(jnp.int32, (count, 2 * LANES), 0) * scale
        return lax.rem(k * orders, NLON).astype(jnp.float32) * unit

    coarse = angle(96, STEP)
    coarse_cos[...] = jnp.cos(coarse)
    coarse_sin[...] = jnp.sin(coarse)
    fine = angle(STEP, 1)
    fine_cos, fine_sin = jnp.cos(fine), jnp.sin(fine)

    @pl.loop(0, NLON // STEP)
    def _(a):
        base_cos, base_sin = coarse_cos[pl.ds(a, 1), :], coarse_sin[pl.ds(a, 1), :]
        even = (base_cos * fine_cos - base_sin * fine_sin).astype(table.dtype)
        odd = (-(base_sin * fine_cos) - base_cos * fine_sin).astype(table.dtype)
        rows = pl.ds(pl.multiple_of(a * STEP, STEP), STEP)
        table[rows, :LANES] = even[:, :LANES]
        table[rows, LANES : 2 * LANES] = odd[:, :LANES]
        table[rows, 2 * LANES : 3 * LANES] = even[:, LANES:]
        table[rows, 3 * LANES :] = odd[:, LANES:]


def forward_kernel(low_ref, x_ref, out_ref, table_ref, product, packed, coarse_cos, coarse_sin):
    @pl.when(pl.program_id(0) == 0)
    def _():
        fill_table(low_ref[...], table_ref, coarse_cos, coarse_sin)
        packed[...] = jnp.zeros_like(packed)

    factor = jnp.where(low_ref[...] == 0, 1.0, 2.0).astype(jnp.float32)

    @pl.loop(0, HALF // CHUNK)
    def _(step):
        first = step * CHUNK
        for half in range(2):
            block = x_ref[0, pl.ds(half * HALF + first, CHUNK)].reshape(CHUNK * CH, NLON)
            product[half] = jnp.dot(block, table_ref[...], preferred_element_type=jnp.float32)
        for t in range(CHUNK):
            rows = slice(t * CH, (t + 1) * CH)
            pieces = []
            for q in range(4):
                scale = factor if q < 2 else 2.0
                for half in range(2):
                    pieces.append(product[half, rows, q * LANES : (q + 1) * LANES] * scale)
            turned = jnp.concatenate(pieces, axis=0).T
            for slot in range(SLOTS):
                packed[pl.ds(slot * HP + first + t, DEST, stride=STRIPE), :] = turned[slot * DEST : (slot + 1) * DEST]

    out_ref[...] = packed[...].astype(out_ref.dtype).reshape(out_ref.shape)


def forward(low, grad):
    return pl.pallas_call(
        forward_kernel,
        grid=(SAMPLES,),
        in_specs=[
            pl.BlockSpec((1, LANES), lambda s: (0, 0)),
            pl.BlockSpec((1, LAT, CH, NLON), lambda s: (s, 0, 0, 0)),
        ],
        out_specs=[
            pl.BlockSpec((DEST, 1, STRIPE, LANES), lambda s: (0, s, 0, 0)),
            pl.BlockSpec((NLON, COLS), lambda s: (0, 0)),
        ],
        out_shape=[
            jax.ShapeDtypeStruct((DEST, SAMPLES, STRIPE, LANES), jnp.bfloat16),
            jax.ShapeDtypeStruct((NLON, COLS), jnp.bfloat16),
        ],
        scratch_shapes=[
            pltpu.VMEM((2, CHUNK * CH, COLS), jnp.float32),
            pltpu.VMEM((DEST * STRIPE, LANES), jnp.float32),
            pltpu.VMEM((96, 2 * LANES), jnp.float32),
            pltpu.VMEM((96, 2 * LANES), jnp.float32),
        ],
        compiler_params=pltpu.CompilerParams(vmem_limit_bytes=VMEM),
        cost_estimate=pl.CostEstimate(flops=2 * 4320 * NLON * COLS, bytes_accessed=18_000_000, transcendentals=0),
        name="forward",
    )(low, grad)


def spectral_kernel(low_ref, z_ref, filt_ref, x_ref, t0, t1, t2, t3, out_ref, legendre, columns, gains, sems):
    step = pl.program_id(0)

    def table_copies():
        copies = []
        for k, source in enumerate((t0, t1, t2, t3)):
            z = lax.rem(z_ref[0] + (4 - k), 4)
            for x_hi in range(2):
                for core in range(2):
                    block = x_hi * 8 + z * 2 + core
                    copies.append(
                        pltpu.make_async_copy(source.at[x_hi * 2 + core], legendre.at[:, block], sems.at[k * 4 + x_hi * 2 + core])
                    )
        return copies

    row = lax.broadcasted_iota(jnp.int32, (1, ROWS), 1)

    @pl.when(step == 0)
    def _():
        for copy in table_copies():
            copy.start()
        for slot in range(SLOTS):
            low = low_ref[slot]
            below = row < M - low
            for part in range(2):
                whole = filt_ref[part]
                gains[slot, part] = jnp.where(below, pltpu.roll(whole, ROWS - low, 1), pltpu.roll(whole, 1, 1))
        for copy in table_copies():
            copy.wait()

    lane = lax.broadcasted_iota(jnp.int32, (HP, LANES), 1)
    former_half = lax.rem(lax.div(lane, CH), 2) == 0

    def shuffle(a, b):
        return jnp.where(former_half, a, pltpu.roll(b, CH, 1)), jnp.where(former_half, pltpu.roll(a, LANES - CH, 1), b)

    for slot in range(SLOTS):
        stripe = slice(slot * HP, (slot + 1) * HP)
        for order in range(8):
            for pair in range(2):
                source = order * GROUPS + pair * 2
                a = x_ref[source, 0, stripe, :].astype(jnp.float32)
                b = x_ref[source + 1, 0, stripe, :].astype(jnp.float32)
                lanes = slice(pair * LANES, (pair + 1) * LANES)
                for half, value in enumerate(shuffle(a, b)):
                    block = order * 2 + half
                    columns[block * HP : (block + 1) * HP, lanes] = value.astype(columns.dtype)
        table = legendre[slot].reshape(16 * HP, ROWS)
        spectrum = lax.dot_general(columns[...], table, TN, preferred_element_type=jnp.float32)
        below = row < M - low_ref[slot]
        parts = []
        for pair in range(2):
            a0, a1, a2, a3 = (spectrum[pair * LANES + q * 32 : pair * LANES + (q + 1) * 32] for q in range(4))
            former, latter = jnp.where(below, a0, a2), jnp.where(below, a1, a3)
            re = gains[slot, 0, pair * 32 : (pair + 1) * 32]
            im = gains[slot, 1, pair * 32 : (pair + 1) * 32]
            real, imag = re * former + im * latter, re * latter - im * former
            parts += [jnp.where(below, real, 0.0), jnp.where(below, imag, 0.0)]
            parts += [jnp.where(below, 0.0, real), jnp.where(below, 0.0, imag)]
        split = jnp.concatenate(parts, axis=0).astype(jnp.bfloat16)
        synthesis = lax.dot_general(table, split, NT, preferred_element_type=jnp.float32)
        for order in range(8):
            for pair in range(2):
                lanes = slice(pair * LANES, (pair + 1) * LANES)
                top, mid = order * 2 * HP, (order * 2 + 1) * HP
                target = order * GROUPS + pair * 2
                for offset, value in enumerate(shuffle(synthesis[top:mid, lanes], synthesis[mid : mid + HP, lanes])):
                    out_ref[target + offset, 0, stripe, :] = value.astype(out_ref.dtype)


def spectral(low, z, filters, received, tables):
    shape = (DEST, SAMPLES, STRIPE, LANES)
    block = pl.BlockSpec((DEST, 1, STRIPE, LANES), lambda s: (0, s, 0, 0))
    smem = pl.BlockSpec(memory_space=pltpu.SMEM)
    hbm = pl.BlockSpec(memory_space=pl.ANY)
    return pl.pallas_call(
        spectral_kernel,
        grid=(SAMPLES,),
        in_specs=[smem, smem, pl.BlockSpec((2, GROUPS * CH, ROWS), lambda s: (0, 0, 0)), block, hbm, hbm, hbm, hbm],
        out_specs=block,
        out_shape=jax.ShapeDtypeStruct(shape, jnp.bfloat16),
        scratch_shapes=[
            pltpu.VMEM((SLOTS, 16, HP, ROWS), jnp.bfloat16),
            pltpu.VMEM((16 * HP, 2 * LANES), jnp.bfloat16),
            pltpu.VMEM((SLOTS, 2, GROUPS * CH, ROWS), jnp.float32),
            pltpu.SemaphoreType.DMA((16,)),
        ],
        compiler_params=pltpu.CompilerParams(vmem_limit_bytes=VMEM),
        cost_estimate=pl.CostEstimate(flops=9 * 4 * ROWS * ROWS * 256, bytes_accessed=12_000_000, transcendentals=0),
        name="spectral",
    )(low, z, filters, received, *tables)


def inverse_kernel(scale_ref, table_ref, x_ref, out_ref, packed, left):
    packed[...] = x_ref[...].astype(jnp.float32).reshape(packed.shape)
    blank = jnp.zeros((LANES - PAIRS, LANES), jnp.float32)

    @pl.loop(0, HALF // CHUNK)
    def _(step):
        first = step * CHUNK
        for t in range(CHUNK):
            pieces = [packed[pl.ds(slot * HP + first + t, DEST, stride=STRIPE), :] for slot in range(SLOTS)]
            turned = jnp.concatenate(pieces + [blank], axis=0).T.astype(left.dtype)
            for q in range(4):
                for half in range(2):
                    piece = turned[(q * 2 + half) * CH : (q * 2 + half + 1) * CH]
                    left[half, t * CH : (t + 1) * CH, q * LANES : (q + 1) * LANES] = piece
        for half in range(2):
            values = lax.dot_general(left[half], table_ref[...], NT, preferred_element_type=jnp.float32)
            for t in range(CHUNK):
                lat = half * HALF + first + t
                out_ref[0, lat] = (values[t * CH : (t + 1) * CH] * scale_ref[lat]).astype(out_ref.dtype)


def inverse(scale, table, received):
    return pl.pallas_call(
        inverse_kernel,
        grid=(SAMPLES,),
        in_specs=[
            pl.BlockSpec(memory_space=pltpu.SMEM),
            pl.BlockSpec((NLON, COLS), lambda s: (0, 0)),
            pl.BlockSpec((DEST, 1, STRIPE, LANES), lambda s: (0, s, 0, 0)),
        ],
        out_specs=pl.BlockSpec((1, LAT, CH, NLON), lambda s: (s, 0, 0, 0)),
        out_shape=jax.ShapeDtypeStruct((SAMPLES, LAT, CH, NLON), jnp.bfloat16),
        scratch_shapes=[
            pltpu.VMEM((DEST * STRIPE, LANES), jnp.float32),
            pltpu.VMEM((2, CHUNK * CH, COLS), jnp.bfloat16),
        ],
        compiler_params=pltpu.CompilerParams(vmem_limit_bytes=VMEM),
        cost_estimate=pl.CostEstimate(flops=2 * 4320 * NLON * COLS, bytes_accessed=18_000_000, transcendentals=0),
        name="inverse",
    )(scale, table, received)


def body(grad_out, legendre, filter_re, filter_im, quad_weight, pair_order):
    group = lax.axis_index("x_hi") * 2 + lax.axis_index("core")
    z = lax.axis_index("z")
    mine = (lax.axis_index("x_lo") * 4 + lax.axis_index("y")) * GROUPS + group

    padded = jnp.pad(legendre, ((0, 0), (0, HP - HALF), (0, 0))).reshape(GROUPS, SLOTS, HP, ROWS)
    own = lax.all_to_all(padded, ("x_hi", "core"), 0, 0)
    tables = [own]
    for shift in range(1, 4):
        tables.append(lax.ppermute(own, "z", [(i, (i + shift) % 4) for i in range(4)]))

    filters = jnp.pad(jnp.stack([filter_re, filter_im]), ((0, 0), (0, 0), (0, ROWS - M)))
    filters = lax.all_gather(filters, ("x_hi", "core"), axis=1, tiled=True)

    low_lanes = jnp.pad(pair_order.reshape(DEST, SLOTS).T.reshape(1, PAIRS), ((0, 0), (0, LANES - PAIRS)))
    packed, table = forward(low_lanes, jnp.transpose(grad_out, (0, 2, 1, 3)))
    received = lax.all_to_all(packed, SLOT_AXES, 0, 0)
    low = lax.dynamic_slice_in_dim(pair_order, mine * SLOTS, SLOTS)
    bands = spectral(low, z.reshape(1), filters, received, tables)
    received = lax.all_to_all(bands, SLOT_AXES, 0, 0)
    values = inverse(quad_weight * (2.0 * math.pi / NLON), table, received)
    return jnp.transpose(values, (0, 2, 1, 3))


def solution(mesh):
    fine = Mesh(mesh.devices.reshape(2, 4, 2, 4, 2), ("x_lo", "y", "x_hi", "z", "core"))
    order, chan = ("x_lo", "y"), ("x_hi", "z", "core")
    in_specs = (P(None, chan, order, None), P(order, chan, None), P(chan, None), P(chan, None), P(order), P())
    return jax.shard_map(body, mesh=fine, in_specs=in_specs, out_specs=P(None, chan, order, None), check_vma=False)
```

```python
import math

import jax
import jax.numpy as jnp
from jax import lax
from jax.experimental import pallas as pl
from jax.experimental.pallas import tpu as pltpu
from jax.sharding import Mesh
from jax.sharding import PartitionSpec as P

NLON = 1440
M = 720
ROWS = 768
PAIRS = 96
SAMPLES = 3
EARLY = 2
CH = 16
LAT = 90
HALF = 45
HP = 48
DEST = 32
SLOTS = 3
GROUPS = 4
STRIPE = SLOTS * HP
LANES = 128
COLS = 4 * LANES
STEP = 16
CHUNK = 9
VMEM = 63 * 1024 * 1024

SLOT_AXES = ("x_lo", "y", "x_hi", "core")
NT = (((1,), (1,)), ((), ()))
TN = (((0,), (0,)), ((), ()))


def fill_table(low, table, coarse_cos, coarse_sin):
    orders = jnp.concatenate([low, M - 1 - low], axis=1)
    unit = 2.0 * math.pi / NLON

    def angle(count, scale):
        k = lax.broadcasted_iota(jnp.int32, (count, 2 * LANES), 0) * scale
        return lax.rem(k * orders, NLON).astype(jnp.float32) * unit

    coarse = angle(96, STEP)
    coarse_cos[...] = jnp.cos(coarse)
    coarse_sin[...] = jnp.sin(coarse)
    fine = angle(STEP, 1)
    fine_cos, fine_sin = jnp.cos(fine), jnp.sin(fine)

    @pl.loop(0, NLON // STEP)
    def _(a):
        base_cos, base_sin = coarse_cos[pl.ds(a, 1), :], coarse_sin[pl.ds(a, 1), :]
        even = (base_cos * fine_cos - base_sin * fine_sin).astype(table.dtype)
        odd = (-(base_sin * fine_cos) - base_cos * fine_sin).astype(table.dtype)
        rows = pl.ds(pl.multiple_of(a * STEP, STEP), STEP)
        table[rows, :LANES] = even[:, :LANES]
        table[rows, LANES : 2 * LANES] = odd[:, :LANES]
        table[rows, 2 * LANES : 3 * LANES] = even[:, LANES:]
        table[rows, 3 * LANES :] = odd[:, LANES:]


def first_forward_kernel(low_ref, x_ref, out_ref, table_ref, product, packed, coarse_cos, coarse_sin):
    @pl.when(pl.program_id(0) == 0)
    def _():
        fill_table(low_ref[...], table_ref, coarse_cos, coarse_sin)
        packed[...] = jnp.zeros_like(packed)

    transform(low_ref, x_ref, table_ref, out_ref, product, packed)


def later_forward_kernel(low_ref, x_ref, table_ref, out_ref, product, packed):
    @pl.when(pl.program_id(0) == 0)
    def _():
        packed[...] = jnp.zeros_like(packed)

    transform(low_ref, x_ref, table_ref, out_ref, product, packed)


def transform(low_ref, x_ref, table_ref, out_ref, product, packed):
    factor = jnp.where(low_ref[...] == 0, 1.0, 2.0).astype(jnp.float32)

    @pl.loop(0, 2)
    def _(half):
        block = x_ref[0, pl.ds(half * HALF, HALF)].reshape(HALF * CH, NLON)
        rows = pl.ds(pl.multiple_of(half * HALF * CH, CH), HALF * CH)
        product[rows, :] = jnp.dot(block, table_ref[...], preferred_element_type=jnp.float32)

    @pl.loop(0, HALF // CHUNK)
    def _(step):
        first = step * CHUNK
        for t in range(CHUNK):
            pieces = []
            for q in range(4):
                scale = factor if q < 2 else 2.0
                for half in range(2):
                    rows = pl.ds(pl.multiple_of((half * HALF + first + t) * CH, CH), CH)
                    pieces.append(product[rows, q * LANES : (q + 1) * LANES] * scale)
            turned = jnp.concatenate(pieces, axis=0).T
            for slot in range(SLOTS):
                packed[pl.ds(slot * HP + first + t, DEST, stride=STRIPE), :] = turned[slot * DEST : (slot + 1) * DEST]

    out_ref[...] = packed[...].astype(out_ref.dtype).reshape(out_ref.shape)


def forward(low, grad, start, count, table=None):
    whole = pl.BlockSpec((NLON, COLS), lambda s: (0, 0))
    in_specs = [pl.BlockSpec((1, LANES), lambda s: (0, 0)), pl.BlockSpec((1, LAT, CH, NLON), lambda s: (s + start, 0, 0, 0))]
    out_specs = [pl.BlockSpec((DEST, 1, STRIPE, LANES), lambda s: (0, s, 0, 0))]
    out_shape = [jax.ShapeDtypeStruct((DEST, count, STRIPE, LANES), jnp.bfloat16)]
    scratch = [pltpu.VMEM((LAT * CH, COLS), jnp.float32), pltpu.VMEM((DEST * STRIPE, LANES), jnp.float32)]
    if table is None:
        out_specs.append(whole)
        out_shape.append(jax.ShapeDtypeStruct((NLON, COLS), jnp.bfloat16))
        scratch += [pltpu.VMEM((96, 2 * LANES), jnp.float32)] * 2
    else:
        in_specs.append(whole)
    return pl.pallas_call(
        first_forward_kernel if table is None else later_forward_kernel,
        grid=(count,),
        in_specs=in_specs,
        out_specs=out_specs,
        out_shape=out_shape,
        scratch_shapes=scratch,
        compiler_params=pltpu.CompilerParams(vmem_limit_bytes=VMEM),
        cost_estimate=pl.CostEstimate(flops=4 * count * 1440 * NLON * COLS, bytes_accessed=count * 6_000_000, transcendentals=0),
        name="forward",
    )(low, grad, *([] if table is None else [table]))


def spectral_kernel(low_ref, place_ref, f0, f1, x_ref, t0, t1, t2, t3, out_ref, legendre, columns, split, synthesis, gains, sems):
    slot = pl.program_id(0)
    group, z = place_ref[0], place_ref[1]

    def table_copies(which):
        copies = []
        for k in range(GROUPS):
            other = jnp.bitwise_xor(group, k)
            for shift, source in enumerate((t0, t1, t2, t3)):
                block = lax.div(other, 2) * 8 + lax.rem(z + (4 - shift), 4) * 2 + lax.rem(other, 2)
                copies.append(pltpu.make_async_copy(source.at[k, which], legendre.at[which, block], sems.at[which, k * 4 + shift]))
        return copies

    @pl.when(slot == 0)
    def _():
        for which in range(SLOTS):
            for copy in table_copies(which):
                copy.start()

    low = low_ref[slot]
    below = lax.broadcasted_iota(jnp.int32, (1, ROWS), 1) < M - low
    for k in range(GROUPS):
        rows = pl.ds(pl.multiple_of(jnp.bitwise_xor(group, k) * CH, CH), CH)
        for part in range(2):
            whole = (f1 if k % 2 else f0)[k // 2, part]
            gains[part, rows, :] = jnp.where(below, pltpu.roll(whole, ROWS - low, 1), pltpu.roll(whole, 1, 1))

    lane = lax.broadcasted_iota(jnp.int32, (HP, LANES), 1)
    former_half = lax.rem(lax.div(lane, CH), 2) == 0

    def shuffle(a, b):
        return jnp.where(former_half, a, pltpu.roll(b, CH, 1)), jnp.where(former_half, pltpu.roll(a, LANES - CH, 1), b)

    samples = x_ref.shape[1]
    tiles = [(sample, pair, slice((sample * 2 + pair) * LANES, (sample * 2 + pair + 1) * LANES)) for sample in range(samples) for pair in range(2)]

    @pl.loop(0, 8)
    def _(order):
        for sample, pair, lanes in tiles:
            a = x_ref[order * GROUPS + pair * 2, sample].astype(jnp.float32)
            b = x_ref[order * GROUPS + pair * 2 + 1, sample].astype(jnp.float32)
            for half, value in enumerate(shuffle(a, b)):
                rows = pl.ds(pl.multiple_of((order * 2 + half) * HP, HP), HP)
                columns[rows, lanes] = value.astype(columns.dtype)

    for copy in table_copies(slot):
        copy.wait()
    table = legendre[slot].reshape(16 * HP, ROWS)
    spectrum = lax.dot_general(columns[...], table, TN, preferred_element_type=jnp.float32)
    for sample, pair, lanes in tiles:
        a0, a1, a2, a3 = (spectrum[lanes.start + q * 32 : lanes.start + (q + 1) * 32] for q in range(4))
        former, latter = jnp.where(below, a0, a2), jnp.where(below, a1, a3)
        re = gains[0, pair * 32 : (pair + 1) * 32]
        im = gains[1, pair * 32 : (pair + 1) * 32]
        real, imag = re * former + im * latter, re * latter - im * former
        parts = (jnp.where(below, real, 0.0), jnp.where(below, imag, 0.0), jnp.where(below, 0.0, real), jnp.where(below, 0.0, imag))
        for q in range(4):
            split[lanes.start + q * 32 : lanes.start + (q + 1) * 32, :] = parts[q].astype(split.dtype)
    synthesis[...] = lax.dot_general(table, split[...], NT, preferred_element_type=jnp.float32)

    @pl.loop(0, 8)
    def _(order):
        for sample, pair, lanes in tiles:
            halves = [synthesis[pl.ds(pl.multiple_of((order * 2 + half) * HP, HP), HP), lanes] for half in range(2)]
            for offset, value in enumerate(shuffle(*halves)):
                out_ref[order * GROUPS + pair * 2 + offset, sample] = value.astype(out_ref.dtype)


def spectral(low, place, filters, received, tables):
    count = received.shape[1]
    width = count * 2 * LANES
    block = pl.BlockSpec((DEST, count, HP, LANES), lambda slot: (0, 0, slot, 0))
    smem = pl.BlockSpec(memory_space=pltpu.SMEM)
    hbm = pl.BlockSpec(memory_space=pl.ANY)
    gain = pl.BlockSpec((2, 2, CH, ROWS), lambda slot: (0, 0, 0, 0))
    return pl.pallas_call(
        spectral_kernel,
        grid=(SLOTS,),
        in_specs=[smem, smem] + [gain] * 2 + [block] + [hbm] * 4,
        out_specs=block,
        out_shape=jax.ShapeDtypeStruct(received.shape, jnp.bfloat16),
        scratch_shapes=[
            pltpu.VMEM((SLOTS, 16, HP, ROWS), jnp.bfloat16),
            pltpu.VMEM((16 * HP, width), jnp.bfloat16),
            pltpu.VMEM((width, ROWS), jnp.bfloat16),
            pltpu.VMEM((16 * HP, width), jnp.float32),
            pltpu.VMEM((2, GROUPS * CH, ROWS), jnp.float32),
            pltpu.SemaphoreType.DMA((SLOTS, 16)),
        ],
        compiler_params=pltpu.CompilerParams(vmem_limit_bytes=VMEM),
        cost_estimate=pl.CostEstimate(flops=12 * ROWS * ROWS * width, bytes_accessed=12_000_000, transcendentals=0),
        name="spectral",
    )(low, place, *filters, received, *tables)


def later_inverse_kernel(scale_ref, table_ref, x_ref, done_ref, out_ref, packed, left):
    inverse_kernel(scale_ref, table_ref, x_ref, out_ref, packed, left)


def inverse_kernel(scale_ref, table_ref, x_ref, out_ref, packed, left):
    packed[...] = x_ref[...].astype(jnp.float32).reshape(packed.shape)
    blank = jnp.zeros((LANES - PAIRS, LANES), jnp.float32)

    @pl.loop(0, HALF // CHUNK)
    def _(step):
        first = step * CHUNK
        for t in range(CHUNK):
            pieces = [packed[pl.ds(slot * HP + first + t, DEST, stride=STRIPE), :] for slot in range(SLOTS)]
            turned = jnp.concatenate(pieces + [blank], axis=0).T.astype(left.dtype)
            for q in range(4):
                for half in range(2):
                    piece = turned[(q * 2 + half) * CH : (q * 2 + half + 1) * CH]
                    rows = pl.ds(pl.multiple_of((half * HALF + first + t) * CH, CH), CH)
                    left[rows, q * LANES : (q + 1) * LANES] = piece

    @pl.loop(0, 2)
    def _(half):
        rows = pl.ds(pl.multiple_of(half * HALF * CH, CH), HALF * CH)
        scale = scale_ref[pl.ds(half * HALF, HALF)]
        for start in range(0, NLON, 512):
            stop = min(start + 512, NLON)
            values = lax.dot_general(left[rows, :], table_ref[start:stop, :], NT, preferred_element_type=jnp.float32)
            values = values.reshape(HALF, CH, stop - start) * scale[:, :, : stop - start]
            out_ref[0, pl.ds(half * HALF, HALF), :, start:stop] = values.astype(out_ref.dtype)


def inverse(scale, table, received, start, done=None):
    count = received.shape[1]
    in_specs = [
        pl.BlockSpec((LAT, 1, 512), lambda s: (0, 0, 0)),
        pl.BlockSpec((NLON, COLS), lambda s: (0, 0)),
        pl.BlockSpec((DEST, 1, STRIPE, LANES), lambda s: (0, s, 0, 0)),
    ]
    return pl.pallas_call(
        inverse_kernel if done is None else later_inverse_kernel,
        grid=(count,),
        in_specs=in_specs if done is None else in_specs + [pl.BlockSpec(memory_space=pl.ANY)],
        out_specs=pl.BlockSpec((1, LAT, CH, NLON), lambda s: (s + start, 0, 0, 0)),
        out_shape=jax.ShapeDtypeStruct((SAMPLES, LAT, CH, NLON), jnp.bfloat16),
        input_output_aliases={} if done is None else {3: 0},
        scratch_shapes=[
            pltpu.VMEM((DEST * STRIPE, LANES), jnp.float32),
            pltpu.VMEM((LAT * CH, COLS), jnp.bfloat16),
        ],
        compiler_params=pltpu.CompilerParams(vmem_limit_bytes=VMEM),
        cost_estimate=pl.CostEstimate(flops=4 * count * 1440 * NLON * COLS, bytes_accessed=count * 6_000_000, transcendentals=0),
        name="inverse",
    )(scale, table, received, *([] if done is None else [done]))


def body(grad_out, legendre, filter_re, filter_im, quad_weight, pair_order):
    group = lax.axis_index("x_hi") * 2 + lax.axis_index("core")
    z = lax.axis_index("z")
    mine = (lax.axis_index("x_lo") * 4 + lax.axis_index("y")) * GROUPS + group

    by_group = legendre.reshape(GROUPS, SLOTS, HALF, ROWS)
    pieces = []
    for k in range(GROUPS):
        piece = lax.dynamic_index_in_dim(by_group, jnp.bitwise_xor(group, k), 0, keepdims=False)
        pieces.append(lax.ppermute(piece, ("x_hi", "core"), [(i, i ^ k) for i in range(GROUPS)]) if k else piece)
    filters = jnp.pad(jnp.stack([filter_re, filter_im]), ((0, 0), (0, 0), (0, ROWS - M)))
    filters = [filters, lax.ppermute(filters, "x_hi", [(0, 1), (1, 0)])]

    low_lanes = jnp.pad(pair_order.reshape(DEST, SLOTS).T.reshape(1, PAIRS), ((0, 0), (0, LANES - PAIRS)))
    grad = jnp.transpose(grad_out, (0, 2, 1, 3))
    packed, table = forward(low_lanes, grad, 0, EARLY)
    packed, pieces, filters = lax.optimization_barrier((packed, pieces, filters))
    early = lax.all_to_all(packed, SLOT_AXES, 0, 0)
    own = jnp.pad(jnp.stack(pieces), ((0, 0), (0, 0), (0, HP - HALF), (0, 0)))
    near = jnp.stack(filters)
    tables = [own] + [lax.ppermute(own, "z", [(i, (i + shift) % 4) for i in range(4)]) for shift in range(1, 4)]
    (packed,) = forward(low_lanes, grad, EARLY, SAMPLES - EARLY, table)
    filters = [near, lax.ppermute(near, "core", [(0, 1), (1, 0)])]
    late = lax.all_to_all(packed, SLOT_AXES, 0, 0)

    low = lax.dynamic_slice_in_dim(pair_order, mine * SLOTS, SLOTS)
    place = jnp.stack([group, z])
    early = lax.all_to_all(spectral(low, place, filters, early, tables), SLOT_AXES, 0, 0)
    late = lax.all_to_all(spectral(low, place, filters, late, tables), SLOT_AXES, 0, 0)

    scale = jnp.broadcast_to((quad_weight * (2.0 * math.pi / NLON))[:, None, None], (LAT, 1, 512))
    values = inverse(scale, table, early, 0)
    values = inverse(scale, table, late, EARLY, values)
    return jnp.transpose(values, (0, 2, 1, 3))


def solution(mesh):
    fine = Mesh(mesh.devices.reshape(2, 4, 2, 4, 2), ("x_lo", "y", "x_hi", "z", "core"))
    order, chan = ("x_lo", "y"), ("x_hi", "z", "core")
    in_specs = (P(None, chan, order, None), P(order, chan, None), P(chan, None), P(chan, None), P(order), P())
    return jax.shard_map(body, mesh=fine, in_specs=in_specs, out_specs=P(None, chan, order, None), check_vma=False)
```

```python
import functools
import math

import jax
import jax.numpy as jnp
from jax import lax
from jax.experimental import pallas as pl
from jax.experimental.pallas import tpu as pltpu
from jax.sharding import Mesh
from jax.sharding import PartitionSpec as P

NLON = 1440
M = 720
ROWS = 768
PAIRS = 96
SAMPLES = 3
EARLY = 2
EXTRA = 8
CH = 16
LAT = 90
HALF = 45
HP = 48
DEST = 32
SLOTS = 3
GROUPS = 4
LANES = 128
COLS = 4 * LANES
STEP = 16
CHUNK = 9
VMEM = 63 * 1024 * 1024

SLOT_AXES = ("x_lo", "y", "x_hi", "core")
NT = (((1,), (1,)), ((), ()))
TN = (((0,), (0,)), ((), ()))


def packed_rows(count):
    return (SLOTS * count * HALF + 7) // 8 * 8


def fill_table(low, table, coarse_cos, coarse_sin):
    orders = jnp.concatenate([low, M - 1 - low], axis=1)
    unit = 2.0 * math.pi / NLON

    def angle(count, scale):
        k = lax.broadcasted_iota(jnp.int32, (count, 2 * LANES), 0) * scale
        return lax.rem(k * orders, NLON).astype(jnp.float32) * unit

    coarse = angle(96, STEP)
    coarse_cos[...] = jnp.cos(coarse)
    coarse_sin[...] = jnp.sin(coarse)
    fine = angle(STEP, 1)
    fine_cos, fine_sin = jnp.cos(fine), jnp.sin(fine)

    @pl.loop(0, NLON // STEP)
    def _(a):
        base_cos, base_sin = coarse_cos[pl.ds(a, 1), :], coarse_sin[pl.ds(a, 1), :]
        even = (base_cos * fine_cos - base_sin * fine_sin).astype(table.dtype)
        odd = (-(base_sin * fine_cos) - base_cos * fine_sin).astype(table.dtype)
        rows = pl.ds(pl.multiple_of(a * STEP, STEP), STEP)
        table[rows, :LANES] = even[:, :LANES]
        table[rows, LANES : 2 * LANES] = odd[:, :LANES]
        table[rows, 2 * LANES : 3 * LANES] = even[:, LANES:]
        table[rows, 3 * LANES :] = odd[:, LANES:]


def first_forward_kernel(low_ref, x_ref, out_ref, table_ref, product, packed, coarse_cos, coarse_sin):
    @pl.when((pl.program_id(0) == 0) & (pl.program_id(1) == 0))
    def _():
        fill_table(low_ref[...], table_ref, coarse_cos, coarse_sin)
        packed[...] = jnp.zeros_like(packed)

    transform(low_ref, x_ref, table_ref, out_ref, product, packed)


def later_forward_kernel(low_ref, x_ref, table_ref, out_ref, product, packed):
    @pl.when((pl.program_id(0) == 0) & (pl.program_id(1) == 0))
    def _():
        packed[...] = jnp.zeros_like(packed)

    transform(low_ref, x_ref, table_ref, out_ref, product, packed)


def transform(low_ref, x_ref, table_ref, out_ref, product, packed):
    sample, count = pl.program_id(0), pl.num_programs(0)
    rows_each = out_ref.shape[1]
    factor = jnp.where(low_ref[...] == 0, 1.0, 2.0).astype(jnp.float32)

    block = x_ref[0].reshape(HALF * CH, NLON)
    rows = pl.ds(pl.multiple_of(pl.program_id(1) * HALF * CH, CH), HALF * CH)
    product[rows, :] = jnp.dot(block, table_ref[...], preferred_element_type=jnp.float32)

    @pl.when(pl.program_id(1) == 1)
    def _():
        @pl.loop(0, HALF // CHUNK)
        def _(step):
            first = step * CHUNK
            for t in range(CHUNK):
                pieces = []
                for q in range(4):
                    scale = factor if q < 2 else 2.0
                    for half in range(2):
                        rows = pl.ds(pl.multiple_of((half * HALF + first + t) * CH, CH), CH)
                        pieces.append(product[rows, q * LANES : (q + 1) * LANES] * scale)
                turned = jnp.concatenate(pieces, axis=0).T
                for slot in range(SLOTS):
                    row = (slot * count + sample) * HALF + first + t
                    packed[pl.ds(row, DEST, stride=rows_each), :] = turned[slot * DEST : (slot + 1) * DEST]

    @pl.when((sample == count - 1) & (pl.program_id(1) == 1))
    def _():
        for device in range(DEST):
            out_ref[device] = packed[device * rows_each : (device + 1) * rows_each, :].astype(out_ref.dtype)


def forward(low, grad, start, count, table=None):
    whole = pl.BlockSpec((NLON, COLS), lambda s, half: (0, 0))
    in_specs = [
        pl.BlockSpec((1, LANES), lambda s, half: (0, 0)),
        pl.BlockSpec((1, HALF, CH, NLON), lambda s, half: (s + start, half, 0, 0)),
    ]
    shape = (DEST, packed_rows(count), LANES)
    out_specs = [pl.BlockSpec(shape, lambda s, half: (0, 0, 0))]
    out_shape = [jax.ShapeDtypeStruct(shape, jnp.bfloat16)]
    scratch = [pltpu.VMEM((LAT * CH, COLS), jnp.float32), pltpu.VMEM((DEST * packed_rows(count), LANES), jnp.float32)]
    if table is None:
        out_specs.append(whole)
        out_shape.append(jax.ShapeDtypeStruct((NLON, COLS), jnp.bfloat16))
        scratch += [pltpu.VMEM((96, 2 * LANES), jnp.float32)] * 2
    else:
        in_specs.append(whole)
    return pl.pallas_call(
        first_forward_kernel if table is None else later_forward_kernel,
        grid=(count, 2),
        in_specs=in_specs,
        out_specs=out_specs,
        out_shape=out_shape,
        scratch_shapes=scratch,
        compiler_params=pltpu.CompilerParams(vmem_limit_bytes=VMEM),
        cost_estimate=pl.CostEstimate(flops=4 * count * 1440 * NLON * COLS, bytes_accessed=count * 6_000_000, transcendentals=0),
        name="forward",
    )(low, grad, *([] if table is None else [table]))


def spectral_kernel(count, low_ref, place_ref, f0, f1, x_ref, t0, t1, t2, t3, out_ref, legendre, columns, split, synthesis, gains, wide, sems):
    slot = pl.program_id(0)
    group, z = place_ref[0], place_ref[1]

    rows_each = x_ref.shape[1]

    def table_copies(which):
        copies = []
        for other in range(GROUPS):
            for shift, source in enumerate((t0, t1, t2, t3)):
                block = other // 2 * 8 + lax.rem(z + (4 - shift), 4) * 2 + other % 2
                copies.append(pltpu.make_async_copy(source.at[other, which], legendre.at[which, block], sems.at[which, other * 4 + shift]))
        return copies

    @pl.when(slot == 0)
    def _():
        for which in range(SLOTS):
            for copy in table_copies(which):
                copy.start()
        for device in range(DEST):
            wide[device * rows_each : (device + 1) * rows_each, :] = x_ref[device].astype(jnp.float32)
        wide[DEST * rows_each :, :] = jnp.zeros((EXTRA, LANES), jnp.float32)

    low = low_ref[slot]
    below = lax.broadcasted_iota(jnp.int32, (1, ROWS), 1) < M - low
    for k in range(GROUPS):
        rows = pl.ds(pl.multiple_of(jnp.bitwise_xor(group, k) * CH, CH), CH)
        for part in range(2):
            whole = (f1 if k % 2 else f0)[k // 2, part]
            gains[part, rows, :] = jnp.where(below, pltpu.roll(whole, ROWS - low, 1), pltpu.roll(whole, 1, 1))

    lane = lax.broadcasted_iota(jnp.int32, (HP, LANES), 1)
    former_half = lax.rem(lax.div(lane, CH), 2) == 0

    def shuffle(a, b):
        return jnp.where(former_half, a, pltpu.roll(b, CH, 1)), jnp.where(former_half, pltpu.roll(a, LANES - CH, 1), b)

    tiles = [(sample, pair, slice((sample * 2 + pair) * LANES, (sample * 2 + pair + 1) * LANES)) for sample in range(count) for pair in range(2)]

    def place(order, pair, offset, sample):
        return (order * GROUPS + pair * 2 + offset) * rows_each + (slot * count + sample) * HALF

    @pl.loop(0, 8)
    def _(order):
        for sample, pair, lanes in tiles:
            a, b = (wide[pl.ds(place(order, pair, offset, sample), HP), :] for offset in range(2))
            for half, value in enumerate(shuffle(a, b)):
                rows = pl.ds(pl.multiple_of((order * 2 + half) * HP, HP), HP)
                columns[rows, lanes] = value.astype(columns.dtype)

    for copy in table_copies(slot):
        copy.wait()
    table = legendre[slot].reshape(16 * HP, ROWS)
    spectrum = lax.dot_general(columns[...], table, TN, preferred_element_type=jnp.float32)
    for sample, pair, lanes in tiles:
        a0, a1, a2, a3 = (spectrum[lanes.start + q * 32 : lanes.start + (q + 1) * 32] for q in range(4))
        former, latter = jnp.where(below, a0, a2), jnp.where(below, a1, a3)
        re = gains[0, pair * 32 : (pair + 1) * 32]
        im = gains[1, pair * 32 : (pair + 1) * 32]
        real, imag = re * former + im * latter, re * latter - im * former
        parts = (jnp.where(below, real, 0.0), jnp.where(below, imag, 0.0), jnp.where(below, 0.0, real), jnp.where(below, 0.0, imag))
        for q in range(4):
            split[lanes.start + q * 32 : lanes.start + (q + 1) * 32, :] = parts[q].astype(split.dtype)
    synthesis[...] = lax.dot_general(table, split[...], NT, preferred_element_type=jnp.float32)

    @pl.loop(0, 8)
    def _(order):
        for sample, pair, lanes in tiles:
            halves = [synthesis[pl.ds(pl.multiple_of((order * 2 + half) * HP, HP), HP), lanes] for half in range(2)]
            for offset, value in enumerate(shuffle(*halves)):
                wide[pl.ds(place(order, pair, offset, sample), HALF), :] = value[:HALF]

    @pl.when(slot == SLOTS - 1)
    def _():
        for device in range(DEST):
            out_ref[device] = wide[device * rows_each : (device + 1) * rows_each, :].astype(out_ref.dtype)


def spectral(low, place, filters, received, tables, count):
    width = count * 2 * LANES
    block = pl.BlockSpec(received.shape, lambda slot: (0, 0, 0))
    smem = pl.BlockSpec(memory_space=pltpu.SMEM)
    hbm = pl.BlockSpec(memory_space=pl.ANY)
    gain = pl.BlockSpec((2, 2, CH, ROWS), lambda slot: (0, 0, 0, 0))
    return pl.pallas_call(
        functools.partial(spectral_kernel, count),
        grid=(SLOTS,),
        in_specs=[smem, smem] + [gain] * 2 + [block] + [hbm] * 4,
        out_specs=block,
        out_shape=jax.ShapeDtypeStruct(received.shape, jnp.bfloat16),
        scratch_shapes=[
            pltpu.VMEM((SLOTS, 16, HP, ROWS), jnp.bfloat16),
            pltpu.VMEM((16 * HP, width), jnp.bfloat16),
            pltpu.VMEM((width, ROWS), jnp.bfloat16),
            pltpu.VMEM((16 * HP, width), jnp.float32),
            pltpu.VMEM((2, GROUPS * CH, ROWS), jnp.float32),
            pltpu.VMEM((DEST * packed_rows(count) + EXTRA, LANES), jnp.float32),
            pltpu.SemaphoreType.DMA((SLOTS, 16)),
        ],
        compiler_params=pltpu.CompilerParams(vmem_limit_bytes=VMEM),
        cost_estimate=pl.CostEstimate(flops=12 * ROWS * ROWS * width, bytes_accessed=12_000_000, transcendentals=0),
        name="spectral",
    )(low, place, *filters, received, *tables)


def later_inverse_kernel(scale_ref, table_ref, x_ref, done_ref, out_ref, packed, left):
    inverse_kernel(scale_ref, table_ref, x_ref, out_ref, packed, left)


def inverse_kernel(scale_ref, table_ref, x_ref, out_ref, packed, left):
    sample, count = pl.program_id(0), pl.num_programs(0)
    rows_each = x_ref.shape[1]

    @pl.when((sample == 0) & (pl.program_id(1) == 0))
    def _():
        for device in range(DEST):
            packed[device * rows_each : (device + 1) * rows_each, :] = x_ref[device].astype(jnp.float32)

    blank = jnp.zeros((LANES - PAIRS, LANES), jnp.float32)

    @pl.when(pl.program_id(1) == 0)
    def _():
        @pl.loop(0, HALF // CHUNK)
        def _(step):
            first = step * CHUNK
            for t in range(CHUNK):
                starts = [(slot * count + sample) * HALF + first + t for slot in range(SLOTS)]
                pieces = [packed[pl.ds(start, DEST, stride=rows_each), :] for start in starts]
                turned = jnp.concatenate(pieces + [blank], axis=0).T.astype(left.dtype)
                for q in range(4):
                    for half in range(2):
                        piece = turned[(q * 2 + half) * CH : (q * 2 + half + 1) * CH]
                        rows = pl.ds(pl.multiple_of((half * HALF + first + t) * CH, CH), CH)
                        left[rows, q * LANES : (q + 1) * LANES] = piece

    rows = pl.ds(pl.multiple_of(pl.program_id(1) * HALF * CH, CH), HALF * CH)
    for start in range(0, NLON, 512):
        stop = min(start + 512, NLON)
        values = lax.dot_general(left[rows, :], table_ref[start:stop, :], NT, preferred_element_type=jnp.float32)
        values = values.reshape(HALF, CH, stop - start) * scale_ref[:, :, : stop - start]
        out_ref[0, :, :, start:stop] = values.astype(out_ref.dtype)


def inverse(scale, table, received, start, count, done=None):
    in_specs = [
        pl.BlockSpec((HALF, 1, 512), lambda s, half: (half, 0, 0)),
        pl.BlockSpec((NLON, COLS), lambda s, half: (0, 0)),
        pl.BlockSpec(received.shape, lambda s, half: (0, 0, 0)),
    ]
    return pl.pallas_call(
        inverse_kernel if done is None else later_inverse_kernel,
        grid=(count, 2),
        in_specs=in_specs if done is None else in_specs + [pl.BlockSpec(memory_space=pl.ANY)],
        out_specs=pl.BlockSpec((1, HALF, CH, NLON), lambda s, half: (s + start, half, 0, 0)),
        out_shape=jax.ShapeDtypeStruct((SAMPLES, LAT, CH, NLON), jnp.bfloat16),
        input_output_aliases={} if done is None else {3: 0},
        scratch_shapes=[
            pltpu.VMEM((DEST * received.shape[1], LANES), jnp.float32),
            pltpu.VMEM((LAT * CH, COLS), jnp.bfloat16),
        ],
        compiler_params=pltpu.CompilerParams(vmem_limit_bytes=VMEM),
        cost_estimate=pl.CostEstimate(flops=4 * count * 1440 * NLON * COLS, bytes_accessed=count * 6_000_000, transcendentals=0),
        name="inverse",
    )(scale, table, received, *([] if done is None else [done]))


def body(grad_out, legendre, filter_re, filter_im, quad_weight, pair_order):
    group = lax.axis_index("x_hi") * 2 + lax.axis_index("core")
    z = lax.axis_index("z")
    mine = (lax.axis_index("x_lo") * 4 + lax.axis_index("y")) * GROUPS + group

    own = lax.all_to_all(legendre.reshape(GROUPS, SLOTS, HALF, ROWS), ("x_hi", "core"), 0, 0)

    filters = jnp.pad(jnp.stack([filter_re, filter_im]), ((0, 0), (0, 0), (0, ROWS - M)))
    far = lax.ppermute(filters, "x_hi", [(0, 1), (1, 0)])

    low_lanes = jnp.pad(pair_order.reshape(DEST, SLOTS).T.reshape(1, PAIRS), ((0, 0), (0, LANES - PAIRS)))
    grad = jnp.transpose(grad_out, (0, 2, 1, 3))
    packed, table = forward(low_lanes, grad, 0, EARLY)
    packed, own, far = lax.optimization_barrier((packed, own, far))
    early = lax.all_to_all(packed, SLOT_AXES, 0, 0)
    own = jnp.pad(own, ((0, 0), (0, 0), (0, HP - HALF), (0, 0)))
    tables = [own] + [lax.ppermute(own, "z", [(i, (i + shift) % 4) for i in range(4)]) for shift in range(1, 4)]
    (packed,) = forward(low_lanes, grad, EARLY, SAMPLES - EARLY, table)
    late = lax.all_to_all(packed, SLOT_AXES, 0, 0)
    near = jnp.stack([filters, far])
    filters = [near, lax.ppermute(near, "core", [(0, 1), (1, 0)])]

    low = lax.dynamic_slice_in_dim(pair_order, mine * SLOTS, SLOTS)
    place = jnp.stack([group, z])
    early = lax.all_to_all(spectral(low, place, filters, early, tables, EARLY), SLOT_AXES, 0, 0)
    late = lax.all_to_all(spectral(low, place, filters, late, tables, SAMPLES - EARLY), SLOT_AXES, 0, 0)

    scale = jnp.broadcast_to((quad_weight * (2.0 * math.pi / NLON))[:, None, None], (LAT, 1, 512))
    values = inverse(scale, table, early, 0, EARLY)
    values = inverse(scale, table, late, EARLY, SAMPLES - EARLY, values)
    return jnp.transpose(values, (0, 2, 1, 3))


def solution(mesh):
    fine = Mesh(mesh.devices.reshape(2, 4, 2, 4, 2), ("x_lo", "y", "x_hi", "z", "core"))
    order, chan = ("x_lo", "y"), ("x_hi", "z", "core")
    in_specs = (P(None, chan, order, None), P(order, chan, None), P(chan, None), P(chan, None), P(order), P())
    return jax.shard_map(body, mesh=fine, in_specs=in_specs, out_specs=P(None, chan, order, None), check_vma=False)
```

```python
import functools
import math

import jax
import jax.numpy as jnp
from jax import lax
from jax.experimental import pallas as pl
from jax.experimental.pallas import tpu as pltpu
from jax.sharding import Mesh
from jax.sharding import PartitionSpec as P

NLON = 1440
M = 720
ROWS = 768
PAIRS = 96
SAMPLES = 3
EARLY = 2
EXTRA = 8
CH = 16
LAT = 90
HALF = 45
HP = 48
DEST = 32
SLOTS = 3
GROUPS = 4
LANES = 128
COLS = 4 * LANES
STEP = 16
CHUNK = 9
VMEM = 63 * 1024 * 1024

SLOT_AXES = ("x_lo", "y", "x_hi", "core")
NT = (((1,), (1,)), ((), ()))
TN = (((0,), (0,)), ((), ()))


def packed_rows(count):
    return (SLOTS * count * HALF + 7) // 8 * 8


def low_lanes(order_ref):
    lane = lax.broadcasted_iota(jnp.int32, (1, LANES), 1)
    low = jnp.zeros((1, LANES), jnp.int32)
    for j in range(PAIRS):
        low = jnp.where(lane == j, order_ref[j % DEST * SLOTS + j // DEST], low)
    return low


def fill_table(low, table, coarse_cos, coarse_sin):
    orders = jnp.concatenate([low, M - 1 - low], axis=1)
    unit = 2.0 * math.pi / NLON

    def angle(count, scale):
        k = lax.broadcasted_iota(jnp.int32, (count, 2 * LANES), 0) * scale
        return lax.rem(k * orders, NLON).astype(jnp.float32) * unit

    coarse = angle(96, STEP)
    coarse_cos[...] = jnp.cos(coarse)
    coarse_sin[...] = jnp.sin(coarse)
    fine = angle(STEP, 1)
    fine_cos, fine_sin = jnp.cos(fine), jnp.sin(fine)

    @pl.loop(0, NLON // STEP)
    def _(a):
        base_cos, base_sin = coarse_cos[pl.ds(a, 1), :], coarse_sin[pl.ds(a, 1), :]
        even = (base_cos * fine_cos - base_sin * fine_sin).astype(table.dtype)
        odd = (-(base_sin * fine_cos) - base_cos * fine_sin).astype(table.dtype)
        rows = pl.ds(pl.multiple_of(a * STEP, STEP), STEP)
        table[rows, :LANES] = even[:, :LANES]
        table[rows, LANES : 2 * LANES] = odd[:, :LANES]
        table[rows, 2 * LANES : 3 * LANES] = even[:, LANES:]
        table[rows, 3 * LANES :] = odd[:, LANES:]


def first_forward_kernel(order_ref, x_ref, out_ref, table_ref, product, packed, factor, coarse_cos, coarse_sin):
    @pl.when((pl.program_id(0) == 0) & (pl.program_id(1) == 0))
    def _():
        low = low_lanes(order_ref)
        fill_table(low, table_ref, coarse_cos, coarse_sin)
        factor[...] = jnp.where(low == 0, 1.0, 2.0).astype(jnp.float32)
        packed[...] = jnp.zeros_like(packed)

    transform(x_ref, table_ref, out_ref, product, packed, factor)


def later_forward_kernel(order_ref, x_ref, table_ref, out_ref, product, packed, factor):
    @pl.when((pl.program_id(0) == 0) & (pl.program_id(1) == 0))
    def _():
        factor[...] = jnp.where(low_lanes(order_ref) == 0, 1.0, 2.0).astype(jnp.float32)
        packed[...] = jnp.zeros_like(packed)

    transform(x_ref, table_ref, out_ref, product, packed, factor)


def transform(x_ref, table_ref, out_ref, product, packed, factor):
    sample, count = pl.program_id(0), pl.num_programs(0)
    rows_each = out_ref.shape[1]

    block = x_ref[0].reshape(HALF * CH, NLON)
    rows = pl.ds(pl.multiple_of(pl.program_id(1) * HALF * CH, CH), HALF * CH)
    product[rows, :] = jnp.dot(block, table_ref[...], preferred_element_type=jnp.float32)

    @pl.when(pl.program_id(1) == 1)
    def _():
        @pl.loop(0, HALF // CHUNK)
        def _(step):
            first = step * CHUNK
            for t in range(CHUNK):
                pieces = []
                for q in range(4):
                    scale = factor[...] if q < 2 else 2.0
                    for half in range(2):
                        rows = pl.ds(pl.multiple_of((half * HALF + first + t) * CH, CH), CH)
                        pieces.append(product[rows, q * LANES : (q + 1) * LANES] * scale)
                turned = jnp.concatenate(pieces, axis=0).T
                for slot in range(SLOTS):
                    row = (slot * count + sample) * HALF + first + t
                    packed[pl.ds(row, DEST, stride=rows_each), :] = turned[slot * DEST : (slot + 1) * DEST]

    @pl.when((sample == count - 1) & (pl.program_id(1) == 1))
    def _():
        for device in range(DEST):
            out_ref[device] = packed[device * rows_each : (device + 1) * rows_each, :].astype(out_ref.dtype)


def forward(pair_order, grad, start, count, table=None):
    whole = pl.BlockSpec((NLON, COLS), lambda s, half: (0, 0))
    in_specs = [
        pl.BlockSpec(memory_space=pltpu.SMEM),
        pl.BlockSpec((1, HALF, CH, NLON), lambda s, half: (s + start, half, 0, 0)),
    ]
    shape = (DEST, packed_rows(count), LANES)
    out_specs = [pl.BlockSpec(shape, lambda s, half: (0, 0, 0))]
    out_shape = [jax.ShapeDtypeStruct(shape, jnp.bfloat16)]
    scratch = [pltpu.VMEM((LAT * CH, COLS), jnp.float32), pltpu.VMEM((DEST * packed_rows(count), LANES), jnp.float32)]
    scratch.append(pltpu.VMEM((1, LANES), jnp.float32))
    if table is None:
        out_specs.append(whole)
        out_shape.append(jax.ShapeDtypeStruct((NLON, COLS), jnp.bfloat16))
        scratch += [pltpu.VMEM((96, 2 * LANES), jnp.float32)] * 2
    else:
        in_specs.append(whole)
    return pl.pallas_call(
        first_forward_kernel if table is None else later_forward_kernel,
        grid=(count, 2),
        in_specs=in_specs,
        out_specs=out_specs,
        out_shape=out_shape,
        scratch_shapes=scratch,
        compiler_params=pltpu.CompilerParams(vmem_limit_bytes=VMEM),
        cost_estimate=pl.CostEstimate(flops=4 * count * 1440 * NLON * COLS, bytes_accessed=count * 6_000_000, transcendentals=0),
        name="forward",
    )(pair_order, grad, *([] if table is None else [table]))


def spectral_kernel(count, low_ref, place_ref, f0, f1, x_ref, t0, t1, t2, t3, out_ref, legendre, columns, split, synthesis, gains, wide, sems):
    slot = pl.program_id(0)
    group, z = place_ref[0], place_ref[1]

    rows_each = x_ref.shape[1]

    def table_copies(which):
        copies = []
        for other in range(GROUPS):
            for shift, source in enumerate((t0, t1, t2, t3)):
                block = other // 2 * 8 + lax.rem(z + (4 - shift), 4) * 2 + other % 2
                copies.append(pltpu.make_async_copy(source.at[other, which], legendre.at[which, block], sems.at[which, other * 4 + shift]))
        return copies

    @pl.when(slot == 0)
    def _():
        for which in range(SLOTS):
            for copy in table_copies(which):
                copy.start()
        for device in range(DEST):
            wide[device * rows_each : (device + 1) * rows_each, :] = x_ref[device].astype(jnp.float32)
        wide[DEST * rows_each :, :] = jnp.zeros((EXTRA, LANES), jnp.float32)

    low = low_ref[slot]
    below = lax.broadcasted_iota(jnp.int32, (1, ROWS), 1) < M - low
    for k in range(GROUPS):
        rows = pl.ds(pl.multiple_of(jnp.bitwise_xor(group, k) * CH, CH), CH)
        for part in range(2):
            whole = (f1 if k % 2 else f0)[k // 2, part]
            gains[part, rows, :] = jnp.where(below, pltpu.roll(whole, ROWS - low, 1), pltpu.roll(whole, 1, 1))

    lane = lax.broadcasted_iota(jnp.int32, (HP, LANES), 1)
    former_half = lax.rem(lax.div(lane, CH), 2) == 0

    def shuffle(a, b):
        return jnp.where(former_half, a, pltpu.roll(b, CH, 1)), jnp.where(former_half, pltpu.roll(a, LANES - CH, 1), b)

    tiles = [(sample, pair, slice((sample * 2 + pair) * LANES, (sample * 2 + pair + 1) * LANES)) for sample in range(count) for pair in range(2)]

    def place(order, pair, offset, sample):
        return (order * GROUPS + pair * 2 + offset) * rows_each + (slot * count + sample) * HALF

    @pl.loop(0, 8)
    def _(order):
        for sample, pair, lanes in tiles:
            a, b = (wide[pl.ds(place(order, pair, offset, sample), HP), :] for offset in range(2))
            for half, value in enumerate(shuffle(a, b)):
                rows = pl.ds(pl.multiple_of((order * 2 + half) * HP, HP), HP)
                columns[rows, lanes] = value.astype(columns.dtype)

    for copy in table_copies(slot):
        copy.wait()
    table = legendre[slot].reshape(16 * HP, ROWS)
    spectrum = lax.dot_general(columns[...], table, TN, preferred_element_type=jnp.float32)
    for sample, pair, lanes in tiles:
        a0, a1, a2, a3 = (spectrum[lanes.start + q * 32 : lanes.start + (q + 1) * 32] for q in range(4))
        former, latter = jnp.where(below, a0, a2), jnp.where(below, a1, a3)
        re = gains[0, pair * 32 : (pair + 1) * 32]
        im = gains[1, pair * 32 : (pair + 1) * 32]
        real, imag = re * former + im * latter, re * latter - im * former
        parts = (jnp.where(below, real, 0.0), jnp.where(below, imag, 0.0), jnp.where(below, 0.0, real), jnp.where(below, 0.0, imag))
        for q in range(4):
            split[lanes.start + q * 32 : lanes.start + (q + 1) * 32, :] = parts[q].astype(split.dtype)
    synthesis[...] = lax.dot_general(table, split[...], NT, preferred_element_type=jnp.float32)

    @pl.loop(0, 8)
    def _(order):
        for sample, pair, lanes in tiles:
            halves = [synthesis[pl.ds(pl.multiple_of((order * 2 + half) * HP, HP), HP), lanes] for half in range(2)]
            for offset, value in enumerate(shuffle(*halves)):
                wide[pl.ds(place(order, pair, offset, sample), HALF), :] = value[:HALF]

    @pl.when(slot == SLOTS - 1)
    def _():
        for device in range(DEST):
            out_ref[device] = wide[device * rows_each : (device + 1) * rows_each, :].astype(out_ref.dtype)


def spectral(low, place, filters, received, tables, count):
    width = count * 2 * LANES
    block = pl.BlockSpec(received.shape, lambda slot: (0, 0, 0))
    smem = pl.BlockSpec(memory_space=pltpu.SMEM)
    hbm = pl.BlockSpec(memory_space=pl.ANY)
    gain = pl.BlockSpec((2, 2, CH, ROWS), lambda slot: (0, 0, 0, 0))
    return pl.pallas_call(
        functools.partial(spectral_kernel, count),
        grid=(SLOTS,),
        in_specs=[smem, smem] + [gain] * 2 + [block] + [hbm] * 4,
        out_specs=block,
        out_shape=jax.ShapeDtypeStruct(received.shape, jnp.bfloat16),
        scratch_shapes=[
            pltpu.VMEM((SLOTS, 16, HP, ROWS), jnp.bfloat16),
            pltpu.VMEM((16 * HP, width), jnp.bfloat16),
            pltpu.VMEM((width, ROWS), jnp.bfloat16),
            pltpu.VMEM((16 * HP, width), jnp.float32),
            pltpu.VMEM((2, GROUPS * CH, ROWS), jnp.float32),
            pltpu.VMEM((DEST * packed_rows(count) + EXTRA, LANES), jnp.float32),
            pltpu.SemaphoreType.DMA((SLOTS, 16)),
        ],
        compiler_params=pltpu.CompilerParams(vmem_limit_bytes=VMEM),
        cost_estimate=pl.CostEstimate(flops=12 * ROWS * ROWS * width, bytes_accessed=12_000_000, transcendentals=0),
        name="spectral",
    )(low, place, *filters, received, *tables)


def later_inverse_kernel(scale_ref, table_ref, x_ref, done_ref, out_ref, packed, left):
    inverse_kernel(scale_ref, table_ref, x_ref, out_ref, packed, left)


def inverse_kernel(scale_ref, table_ref, x_ref, out_ref, packed, left):
    sample, count = pl.program_id(0), pl.num_programs(0)
    rows_each = x_ref.shape[1]

    @pl.when((sample == 0) & (pl.program_id(1) == 0))
    def _():
        for device in range(DEST):
            packed[device * rows_each : (device + 1) * rows_each, :] = x_ref[device].astype(jnp.float32)

    blank = jnp.zeros((LANES - PAIRS, LANES), jnp.float32)

    @pl.when(pl.program_id(1) == 0)
    def _():
        @pl.loop(0, HALF // CHUNK)
        def _(step):
            first = step * CHUNK
            for t in range(CHUNK):
                starts = [(slot * count + sample) * HALF + first + t for slot in range(SLOTS)]
                pieces = [packed[pl.ds(start, DEST, stride=rows_each), :] for start in starts]
                turned = jnp.concatenate(pieces + [blank], axis=0).T.astype(left.dtype)
                for q in range(4):
                    for half in range(2):
                        piece = turned[(q * 2 + half) * CH : (q * 2 + half + 1) * CH]
                        rows = pl.ds(pl.multiple_of((half * HALF + first + t) * CH, CH), CH)
                        left[rows, q * LANES : (q + 1) * LANES] = piece

    rows = pl.ds(pl.multiple_of(pl.program_id(1) * HALF * CH, CH), HALF * CH)
    for start in range(0, NLON, 512):
        stop = min(start + 512, NLON)
        values = lax.dot_general(left[rows, :], table_ref[start:stop, :], NT, preferred_element_type=jnp.float32)
        values = values.reshape(HALF, CH, stop - start) * scale_ref[:, :, : stop - start]
        out_ref[0, :, :, start:stop] = values.astype(out_ref.dtype)


def inverse(scale, table, received, start, count, done=None):
    in_specs = [
        pl.BlockSpec((HALF, 1, 512), lambda s, half: (half, 0, 0)),
        pl.BlockSpec((NLON, COLS), lambda s, half: (0, 0)),
        pl.BlockSpec(received.shape, lambda s, half: (0, 0, 0)),
    ]
    return pl.pallas_call(
        inverse_kernel if done is None else later_inverse_kernel,
        grid=(count, 2),
        in_specs=in_specs if done is None else in_specs + [pl.BlockSpec(memory_space=pl.ANY)],
        out_specs=pl.BlockSpec((1, HALF, CH, NLON), lambda s, half: (s + start, half, 0, 0)),
        out_shape=jax.ShapeDtypeStruct((SAMPLES, LAT, CH, NLON), jnp.bfloat16),
        input_output_aliases={} if done is None else {3: 0},
        scratch_shapes=[
            pltpu.VMEM((DEST * received.shape[1], LANES), jnp.float32),
            pltpu.VMEM((LAT * CH, COLS), jnp.bfloat16),
        ],
        compiler_params=pltpu.CompilerParams(vmem_limit_bytes=VMEM),
        cost_estimate=pl.CostEstimate(flops=4 * count * 1440 * NLON * COLS, bytes_accessed=count * 6_000_000, transcendentals=0),
        name="inverse",
    )(scale, table, received, *([] if done is None else [done]))


def padded_filters(filter_re, filter_im):
    return jnp.pad(jnp.stack([filter_re, filter_im]), ((0, 0), (0, 0), (0, ROWS - M)))


def body(grad_out, legendre, filter_re, filter_im, quad_weight, pair_order):
    group = lax.axis_index("x_hi") * 2 + lax.axis_index("core")
    z = lax.axis_index("z")
    mine = (lax.axis_index("x_lo") * 4 + lax.axis_index("y")) * GROUPS + group

    own = lax.all_to_all(legendre.reshape(GROUPS, SLOTS, HALF, ROWS), ("x_hi", "core"), 0, 0)

    far = lax.ppermute(padded_filters(filter_re, filter_im), "x_hi", [(0, 1), (1, 0)])

    grad = jnp.transpose(grad_out, (0, 2, 1, 3))
    packed, table = forward(pair_order, grad, 0, EARLY)
    packed, own, far, filter_re, filter_im = lax.optimization_barrier((packed, own, far, filter_re, filter_im))
    early = lax.all_to_all(packed, SLOT_AXES, 0, 0)
    own = jnp.pad(own, ((0, 0), (0, 0), (0, HP - HALF), (0, 0)))
    tables = [own] + [lax.ppermute(own, "z", [(i, (i + shift) % 4) for i in range(4)]) for shift in range(1, 4)]
    (packed,) = forward(pair_order, grad, EARLY, SAMPLES - EARLY, table)
    late = lax.all_to_all(packed, SLOT_AXES, 0, 0)
    near = jnp.stack([padded_filters(filter_re, filter_im), far])
    filters = [near, lax.ppermute(near, "core", [(0, 1), (1, 0)])]

    low = lax.dynamic_slice_in_dim(pair_order, mine * SLOTS, SLOTS)
    place = jnp.stack([group, z])
    early = lax.all_to_all(spectral(low, place, filters, early, tables, EARLY), SLOT_AXES, 0, 0)
    late = lax.all_to_all(spectral(low, place, filters, late, tables, SAMPLES - EARLY), SLOT_AXES, 0, 0)

    scale = jnp.broadcast_to((quad_weight * (2.0 * math.pi / NLON))[:, None, None], (LAT, 1, 512))
    values = inverse(scale, table, early, 0, EARLY)
    values = inverse(scale, table, late, EARLY, SAMPLES - EARLY, values)
    return jnp.transpose(values, (0, 2, 1, 3))


def solution(mesh):
    fine = Mesh(mesh.devices.reshape(2, 4, 2, 4, 2), ("x_lo", "y", "x_hi", "z", "core"))
    order, chan = ("x_lo", "y"), ("x_hi", "z", "core")
    in_specs = (P(None, chan, order, None), P(order, chan, None), P(chan, None), P(chan, None), P(order), P())
    return jax.shard_map(body, mesh=fine, in_specs=in_specs, out_specs=P(None, chan, order, None), check_vma=False)
```

```python
import functools
import math

import jax
import jax.numpy as jnp
from jax import lax
from jax.experimental import pallas as pl
from jax.experimental.pallas import tpu as pltpu
from jax.sharding import Mesh
from jax.sharding import PartitionSpec as P

NLON = 1440
M = 720
ROWS = 768
PAIRS = 96
SAMPLES = 3
EARLY = 2
EXTRA = 8
CH = 16
LAT = 90
HALF = 45
HP = 48
DEST = 32
SLOTS = 3
GROUPS = 4
LANES = 128
COLS = 4 * LANES
STEP = 16
CHUNK = 9
VMEM = 63 * 1024 * 1024

SLOT_AXES = ("x_lo", "y", "x_hi", "core")
NT = (((1,), (1,)), ((), ()))
TN = (((0,), (0,)), ((), ()))


def packed_rows(count):
    return (SLOTS * count * HALF + 7) // 8 * 8


def low_lanes(order_ref):
    lane = lax.broadcasted_iota(jnp.int32, (1, LANES), 1)
    low = jnp.zeros((1, LANES), jnp.int32)
    for j in range(PAIRS):
        low = jnp.where(lane == j, order_ref[j % DEST * SLOTS + j // DEST], low)
    return low


def fill_table(low, table, coarse_cos, coarse_sin):
    orders = jnp.concatenate([low, M - 1 - low], axis=1)
    unit = 2.0 * math.pi / NLON

    def angle(count, scale):
        k = lax.broadcasted_iota(jnp.int32, (count, 2 * LANES), 0) * scale
        return lax.rem(k * orders, NLON).astype(jnp.float32) * unit

    coarse = angle(96, STEP)
    coarse_cos[...] = jnp.cos(coarse)
    coarse_sin[...] = jnp.sin(coarse)
    fine = angle(STEP, 1)
    fine_cos, fine_sin = jnp.cos(fine), jnp.sin(fine)

    @pl.loop(0, NLON // STEP)
    def _(a):
        base_cos, base_sin = coarse_cos[pl.ds(a, 1), :], coarse_sin[pl.ds(a, 1), :]
        even = (base_cos * fine_cos - base_sin * fine_sin).astype(table.dtype)
        odd = (-(base_sin * fine_cos) - base_cos * fine_sin).astype(table.dtype)
        rows = pl.ds(pl.multiple_of(a * STEP, STEP), STEP)
        table[rows, :LANES] = even[:, :LANES]
        table[rows, LANES : 2 * LANES] = odd[:, :LANES]
        table[rows, 2 * LANES : 3 * LANES] = even[:, LANES:]
        table[rows, 3 * LANES :] = odd[:, LANES:]


def first_forward_kernel(order_ref, x_ref, out_ref, table_ref, product, packed, factor, coarse_cos, coarse_sin):
    @pl.when((pl.program_id(0) == 0) & (pl.program_id(1) == 0))
    def _():
        low = low_lanes(order_ref)
        fill_table(low, table_ref, coarse_cos, coarse_sin)
        factor[...] = jnp.where(low == 0, 1.0, 2.0).astype(jnp.float32)
        packed[...] = jnp.zeros_like(packed)

    transform(x_ref, table_ref, out_ref, product, packed, factor)


def later_forward_kernel(order_ref, x_ref, table_ref, out_ref, product, packed, factor):
    @pl.when((pl.program_id(0) == 0) & (pl.program_id(1) == 0))
    def _():
        factor[...] = jnp.where(low_lanes(order_ref) == 0, 1.0, 2.0).astype(jnp.float32)
        packed[...] = jnp.zeros_like(packed)

    transform(x_ref, table_ref, out_ref, product, packed, factor)


def transform(x_ref, table_ref, out_ref, product, packed, factor):
    sample, count = pl.program_id(0), pl.num_programs(0)
    rows_each = out_ref.shape[1]

    block = x_ref[0].reshape(HALF * CH, NLON)
    rows = pl.ds(pl.multiple_of(pl.program_id(1) * HALF * CH, CH), HALF * CH)
    product[rows, :] = jnp.dot(block, table_ref[...], preferred_element_type=jnp.float32)

    @pl.when(pl.program_id(1) == 1)
    def _():
        @pl.loop(0, HALF // CHUNK)
        def _(step):
            first = step * CHUNK
            for t in range(CHUNK):
                pieces = []
                for q in range(4):
                    scale = factor[...] if q < 2 else 2.0
                    for half in range(2):
                        rows = pl.ds(pl.multiple_of((half * HALF + first + t) * CH, CH), CH)
                        pieces.append(product[rows, q * LANES : (q + 1) * LANES] * scale)
                turned = jnp.concatenate(pieces, axis=0).T
                for slot in range(SLOTS):
                    row = (slot * count + sample) * HALF + first + t
                    packed[pl.ds(row, DEST, stride=rows_each), :] = turned[slot * DEST : (slot + 1) * DEST]

    @pl.when((sample == count - 1) & (pl.program_id(1) == 1))
    def _():
        for device in range(DEST):
            out_ref[device] = packed[device * rows_each : (device + 1) * rows_each, :].astype(out_ref.dtype)


def forward(pair_order, grad, start, count, table=None):
    whole = pl.BlockSpec((NLON, COLS), lambda s, half: (0, 0))
    in_specs = [
        pl.BlockSpec(memory_space=pltpu.SMEM),
        pl.BlockSpec((1, HALF, CH, NLON), lambda s, half: (s + start, half, 0, 0)),
    ]
    shape = (DEST, packed_rows(count), LANES)
    out_specs = [pl.BlockSpec(shape, lambda s, half: (0, 0, 0))]
    out_shape = [jax.ShapeDtypeStruct(shape, jnp.bfloat16)]
    scratch = [pltpu.VMEM((LAT * CH, COLS), jnp.float32), pltpu.VMEM((DEST * packed_rows(count), LANES), jnp.float32)]
    scratch.append(pltpu.VMEM((1, LANES), jnp.float32))
    if table is None:
        out_specs.append(whole)
        out_shape.append(jax.ShapeDtypeStruct((NLON, COLS), jnp.bfloat16))
        scratch += [pltpu.VMEM((96, 2 * LANES), jnp.float32)] * 2
    else:
        in_specs.append(whole)
    return pl.pallas_call(
        first_forward_kernel if table is None else later_forward_kernel,
        grid=(count, 2),
        in_specs=in_specs,
        out_specs=out_specs,
        out_shape=out_shape,
        scratch_shapes=scratch,
        compiler_params=pltpu.CompilerParams(vmem_limit_bytes=VMEM),
        cost_estimate=pl.CostEstimate(flops=4 * count * 1440 * NLON * COLS, bytes_accessed=count * 6_000_000, transcendentals=0),
        name="forward",
    )(pair_order, grad, *([] if table is None else [table]))


def place(order, pair, offset, piece, rows_each):
    return (order * GROUPS + pair * 2 + offset) * rows_each + piece * HALF


def column_tiles(count):
    return [
        (sample, pair, slice((sample * 2 + pair) * LANES, (sample * 2 + pair + 1) * LANES))
        for sample in range(count)
        for pair in range(2)
    ]


def shuffle(a, b):
    lane = lax.broadcasted_iota(jnp.int32, (HP, LANES), 1)
    former_half = lax.rem(lax.div(lane, CH), 2) == 0
    return jnp.where(former_half, a, pltpu.roll(b, CH, 1)), jnp.where(former_half, pltpu.roll(a, LANES - CH, 1), b)


def columns_kernel(count, x_ref, out_ref, wide):
    slot = pl.program_id(0)
    rows_each = x_ref.shape[1]

    @pl.when(slot == 0)
    def _():
        for device in range(DEST):
            wide[device * rows_each : (device + 1) * rows_each, :] = x_ref[device].astype(jnp.float32)
        wide[DEST * rows_each :, :] = jnp.zeros((EXTRA, LANES), jnp.float32)

    @pl.loop(0, 8)
    def _(order):
        for sample, pair, lanes in column_tiles(count):
            a, b = (wide[pl.ds(place(order, pair, offset, slot * count + sample, rows_each), HP), :] for offset in range(2))
            for half, value in enumerate(shuffle(a, b)):
                rows = pl.ds(pl.multiple_of((order * 2 + half) * HP, HP), HP)
                out_ref[0, rows, lanes] = value.astype(out_ref.dtype)


def columns_of(received, count):
    width = count * 2 * LANES
    return pl.pallas_call(
        functools.partial(columns_kernel, count),
        grid=(SLOTS,),
        in_specs=[pl.BlockSpec(received.shape, lambda slot: (0, 0, 0))],
        out_specs=pl.BlockSpec((1, 16 * HP, width), lambda slot: (slot, 0, 0)),
        out_shape=jax.ShapeDtypeStruct((SLOTS, 16 * HP, width), jnp.bfloat16),
        scratch_shapes=[pltpu.VMEM((DEST * packed_rows(count) + EXTRA, LANES), jnp.float32)],
        compiler_params=pltpu.CompilerParams(vmem_limit_bytes=VMEM),
        cost_estimate=pl.CostEstimate(flops=10_000_000, bytes_accessed=5_000_000, transcendentals=0),
        name="columns",
    )(received)


def spectral_kernel(count, low_ref, place_ref, f0, f1, columns, t0, t1, t2, t3, out_ref, legendre, split, synthesis, gains, wide, sems):
    slot = pl.program_id(0)
    group, z = place_ref[0], place_ref[1]

    rows_each = out_ref.shape[1]
    tiles = column_tiles(count)

    def table_copies(which):
        copies = []
        for other in range(GROUPS):
            for shift, source in enumerate((t0, t1, t2, t3)):
                block = other // 2 * 8 + lax.rem(z + (4 - shift), 4) * 2 + other % 2
                copies.append(pltpu.make_async_copy(source.at[other, which], legendre.at[which, block], sems.at[which, other * 4 + shift]))
        return copies

    @pl.when(slot == 0)
    def _():
        for which in range(SLOTS):
            for copy in table_copies(which):
                copy.start()
        used = SLOTS * count * HALF
        for device in range(DEST):
            wide[device * rows_each + used : (device + 1) * rows_each, :] = jnp.zeros((rows_each - used, LANES), jnp.float32)

    low = low_ref[slot]
    below = lax.broadcasted_iota(jnp.int32, (1, ROWS), 1) < M - low
    for k in range(GROUPS):
        rows = pl.ds(pl.multiple_of(jnp.bitwise_xor(group, k) * CH, CH), CH)
        for part in range(2):
            whole = (f1 if k % 2 else f0)[k // 2, part]
            gains[part, rows, :] = jnp.where(below, pltpu.roll(whole, ROWS - low, 1), pltpu.roll(whole, 1, 1))

    for copy in table_copies(slot):
        copy.wait()
    table = legendre[slot].reshape(16 * HP, ROWS)
    spectrum = lax.dot_general(columns[0], table, TN, preferred_element_type=jnp.float32)
    for sample, pair, lanes in tiles:
        a0, a1, a2, a3 = (spectrum[lanes.start + q * 32 : lanes.start + (q + 1) * 32] for q in range(4))
        former, latter = jnp.where(below, a0, a2), jnp.where(below, a1, a3)
        re = gains[0, pair * 32 : (pair + 1) * 32]
        im = gains[1, pair * 32 : (pair + 1) * 32]
        real, imag = re * former + im * latter, re * latter - im * former
        parts = (jnp.where(below, real, 0.0), jnp.where(below, imag, 0.0), jnp.where(below, 0.0, real), jnp.where(below, 0.0, imag))
        for q in range(4):
            split[lanes.start + q * 32 : lanes.start + (q + 1) * 32, :] = parts[q].astype(split.dtype)
    synthesis[...] = lax.dot_general(table, split[...], NT, preferred_element_type=jnp.float32)

    @pl.loop(0, 8)
    def _(order):
        for sample, pair, lanes in tiles:
            halves = [synthesis[pl.ds(pl.multiple_of((order * 2 + half) * HP, HP), HP), lanes] for half in range(2)]
            for offset, value in enumerate(shuffle(*halves)):
                wide[pl.ds(place(order, pair, offset, slot * count + sample, rows_each), HALF), :] = value[:HALF]

    @pl.when(slot == SLOTS - 1)
    def _():
        for device in range(DEST):
            out_ref[device] = wide[device * rows_each : (device + 1) * rows_each, :].astype(out_ref.dtype)


def spectral(low, where, filters, received, tables, count):
    width = count * 2 * LANES
    shape = (DEST, packed_rows(count), LANES)
    smem = pl.BlockSpec(memory_space=pltpu.SMEM)
    hbm = pl.BlockSpec(memory_space=pl.ANY)
    gain = pl.BlockSpec((2, 2, CH, ROWS), lambda slot: (0, 0, 0, 0))
    return pl.pallas_call(
        functools.partial(spectral_kernel, count),
        grid=(SLOTS,),
        in_specs=[smem, smem] + [gain] * 2 + [pl.BlockSpec((1, 16 * HP, width), lambda slot: (slot, 0, 0))] + [hbm] * 4,
        out_specs=pl.BlockSpec(shape, lambda slot: (0, 0, 0)),
        out_shape=jax.ShapeDtypeStruct(shape, jnp.bfloat16),
        scratch_shapes=[
            pltpu.VMEM((SLOTS, 16, HP, ROWS), jnp.bfloat16),
            pltpu.VMEM((width, ROWS), jnp.bfloat16),
            pltpu.VMEM((16 * HP, width), jnp.float32),
            pltpu.VMEM((2, GROUPS * CH, ROWS), jnp.float32),
            pltpu.VMEM((DEST * packed_rows(count) + EXTRA, LANES), jnp.float32),
            pltpu.SemaphoreType.DMA((SLOTS, 16)),
        ],
        compiler_params=pltpu.CompilerParams(vmem_limit_bytes=VMEM),
        cost_estimate=pl.CostEstimate(flops=12 * ROWS * ROWS * width, bytes_accessed=12_000_000, transcendentals=0),
        name="spectral",
    )(low, where, *filters, columns_of(received, count), *tables)


def later_inverse_kernel(scale_ref, table_ref, x_ref, done_ref, out_ref, packed, left):
    inverse_kernel(scale_ref, table_ref, x_ref, out_ref, packed, left)


def inverse_kernel(scale_ref, table_ref, x_ref, out_ref, packed, left):
    sample, count = pl.program_id(0), pl.num_programs(0)
    rows_each = x_ref.shape[1]

    @pl.when((sample == 0) & (pl.program_id(1) == 0))
    def _():
        for device in range(DEST):
            packed[device * rows_each : (device + 1) * rows_each, :] = x_ref[device].astype(jnp.float32)

    blank = jnp.zeros((LANES - PAIRS, LANES), jnp.float32)

    @pl.when(pl.program_id(1) == 0)
    def _():
        @pl.loop(0, HALF // CHUNK)
        def _(step):
            first = step * CHUNK
            for t in range(CHUNK):
                starts = [(slot * count + sample) * HALF + first + t for slot in range(SLOTS)]
                pieces = [packed[pl.ds(start, DEST, stride=rows_each), :] for start in starts]
                turned = jnp.concatenate(pieces + [blank], axis=0).T.astype(left.dtype)
                for q in range(4):
                    for half in range(2):
                        piece = turned[(q * 2 + half) * CH : (q * 2 + half + 1) * CH]
                        rows = pl.ds(pl.multiple_of((half * HALF + first + t) * CH, CH), CH)
                        left[rows, q * LANES : (q + 1) * LANES] = piece

    rows = pl.ds(pl.multiple_of(pl.program_id(1) * HALF * CH, CH), HALF * CH)
    for start in range(0, NLON, 512):
        stop = min(start + 512, NLON)
        values = lax.dot_general(left[rows, :], table_ref[start:stop, :], NT, preferred_element_type=jnp.float32)
        values = values.reshape(HALF, CH, stop - start) * scale_ref[:, :, : stop - start]
        out_ref[0, :, :, start:stop] = values.astype(out_ref.dtype)


def inverse(scale, table, received, start, count, done=None):
    in_specs = [
        pl.BlockSpec((HALF, 1, 512), lambda s, half: (half, 0, 0)),
        pl.BlockSpec((NLON, COLS), lambda s, half: (0, 0)),
        pl.BlockSpec(received.shape, lambda s, half: (0, 0, 0)),
    ]
    return pl.pallas_call(
        inverse_kernel if done is None else later_inverse_kernel,
        grid=(count, 2),
        in_specs=in_specs if done is None else in_specs + [pl.BlockSpec(memory_space=pl.ANY)],
        out_specs=pl.BlockSpec((1, HALF, CH, NLON), lambda s, half: (s + start, half, 0, 0)),
        out_shape=jax.ShapeDtypeStruct((SAMPLES, LAT, CH, NLON), jnp.bfloat16),
        input_output_aliases={} if done is None else {3: 0},
        scratch_shapes=[
            pltpu.VMEM((DEST * received.shape[1], LANES), jnp.float32),
            pltpu.VMEM((LAT * CH, COLS), jnp.bfloat16),
        ],
        compiler_params=pltpu.CompilerParams(vmem_limit_bytes=VMEM),
        cost_estimate=pl.CostEstimate(flops=4 * count * 1440 * NLON * COLS, bytes_accessed=count * 6_000_000, transcendentals=0),
        name="inverse",
    )(scale, table, received, *([] if done is None else [done]))


def padded_filters(filter_re, filter_im):
    return jnp.pad(jnp.stack([filter_re, filter_im]), ((0, 0), (0, 0), (0, ROWS - M)))


def body(grad_out, legendre, filter_re, filter_im, quad_weight, pair_order):
    group = lax.axis_index("x_hi") * 2 + lax.axis_index("core")
    z = lax.axis_index("z")
    mine = (lax.axis_index("x_lo") * 4 + lax.axis_index("y")) * GROUPS + group

    own = lax.all_to_all(legendre.reshape(GROUPS, SLOTS, HALF, ROWS), ("x_hi", "core"), 0, 0)

    far = lax.ppermute(padded_filters(filter_re, filter_im), "x_hi", [(0, 1), (1, 0)])

    grad = jnp.transpose(grad_out, (0, 2, 1, 3))
    packed, table = forward(pair_order, grad, 0, EARLY)
    packed, own, far, filter_re, filter_im = lax.optimization_barrier((packed, own, far, filter_re, filter_im))
    early = lax.all_to_all(packed, SLOT_AXES, 0, 0)
    own = jnp.pad(own, ((0, 0), (0, 0), (0, HP - HALF), (0, 0)))
    tables = [own] + [lax.ppermute(own, "z", [(i, (i + shift) % 4) for i in range(4)]) for shift in range(1, 4)]
    (packed,) = forward(pair_order, grad, EARLY, SAMPLES - EARLY, table)
    late = lax.all_to_all(packed, SLOT_AXES, 0, 0)
    near = jnp.stack([padded_filters(filter_re, filter_im), far])
    filters = [near, lax.ppermute(near, "core", [(0, 1), (1, 0)])]

    low = lax.dynamic_slice_in_dim(pair_order, mine * SLOTS, SLOTS)
    where = jnp.stack([group, z])
    early = lax.all_to_all(spectral(low, where, filters, early, tables, EARLY), SLOT_AXES, 0, 0)
    late = lax.all_to_all(spectral(low, where, filters, late, tables, SAMPLES - EARLY), SLOT_AXES, 0, 0)

    scale = jnp.broadcast_to((quad_weight * (2.0 * math.pi / NLON))[:, None, None], (LAT, 1, 512))
    values = inverse(scale, table, early, 0, EARLY)
    values = inverse(scale, table, late, EARLY, SAMPLES - EARLY, values)
    return jnp.transpose(values, (0, 2, 1, 3))


def solution(mesh):
    fine = Mesh(mesh.devices.reshape(2, 4, 2, 4, 2), ("x_lo", "y", "x_hi", "z", "core"))
    order, chan = ("x_lo", "y"), ("x_hi", "z", "core")
    in_specs = (P(None, chan, order, None), P(order, chan, None), P(chan, None), P(chan, None), P(order), P())
    return jax.shard_map(body, mesh=fine, in_specs=in_specs, out_specs=P(None, chan, order, None), check_vma=False)
```

```python
import functools
import math

import jax
import jax.numpy as jnp
from jax import lax
from jax.experimental import pallas as pl
from jax.experimental.pallas import tpu as pltpu
from jax.sharding import Mesh
from jax.sharding import PartitionSpec as P

NLON = 1440
M = 720
ROWS = 768
PAIRS = 96
SAMPLES = 3
EARLY = 1
EXTRA = 8
CH = 16
LAT = 90
HALF = 45
HP = 48
DEST = 32
SLOTS = 3
GROUPS = 4
LANES = 128
COLS = 4 * LANES
STEP = 16
CHUNK = 9
VMEM = 63 * 1024 * 1024

SLOT_AXES = ("x_lo", "y", "x_hi", "core")
NT = (((1,), (1,)), ((), ()))
TN = (((0,), (0,)), ((), ()))


def packed_rows(count):
    return (SLOTS * count * HALF + 7) // 8 * 8


def low_lanes(order_ref):
    lane = lax.broadcasted_iota(jnp.int32, (1, LANES), 1)
    low = jnp.zeros((1, LANES), jnp.int32)
    for j in range(PAIRS):
        low = jnp.where(lane == j, order_ref[j % DEST * SLOTS + j // DEST], low)
    return low


def fill_table(low, table, coarse_cos, coarse_sin):
    orders = jnp.concatenate([low, M - 1 - low], axis=1)
    unit = 2.0 * math.pi / NLON

    def angle(count, scale):
        k = lax.broadcasted_iota(jnp.int32, (count, 2 * LANES), 0) * scale
        return lax.rem(k * orders, NLON).astype(jnp.float32) * unit

    coarse = angle(96, STEP)
    coarse_cos[...] = jnp.cos(coarse)
    coarse_sin[...] = jnp.sin(coarse)
    fine = angle(STEP, 1)
    fine_cos, fine_sin = jnp.cos(fine), jnp.sin(fine)

    @pl.loop(0, NLON // STEP)
    def _(a):
        base_cos, base_sin = coarse_cos[pl.ds(a, 1), :], coarse_sin[pl.ds(a, 1), :]
        even = (base_cos * fine_cos - base_sin * fine_sin).astype(table.dtype)
        odd = (-(base_sin * fine_cos) - base_cos * fine_sin).astype(table.dtype)
        rows = pl.ds(pl.multiple_of(a * STEP, STEP), STEP)
        table[rows, :LANES] = even[:, :LANES]
        table[rows, LANES : 2 * LANES] = odd[:, :LANES]
        table[rows, 2 * LANES : 3 * LANES] = even[:, LANES:]
        table[rows, 3 * LANES :] = odd[:, LANES:]


def first_forward_kernel(order_ref, x_ref, out_ref, table_ref, product, packed, factor, coarse_cos, coarse_sin):
    @pl.when((pl.program_id(0) == 0) & (pl.program_id(1) == 0))
    def _():
        low = low_lanes(order_ref)
        fill_table(low, table_ref, coarse_cos, coarse_sin)
        factor[...] = jnp.where(low == 0, 1.0, 2.0).astype(jnp.float32)
        packed[...] = jnp.zeros_like(packed)

    transform(x_ref, table_ref, out_ref, product, packed, factor)


def later_forward_kernel(order_ref, x_ref, table_ref, out_ref, product, packed, factor):
    @pl.when((pl.program_id(0) == 0) & (pl.program_id(1) == 0))
    def _():
        factor[...] = jnp.where(low_lanes(order_ref) == 0, 1.0, 2.0).astype(jnp.float32)
        packed[...] = jnp.zeros_like(packed)

    transform(x_ref, table_ref, out_ref, product, packed, factor)


def transform(x_ref, table_ref, out_ref, product, packed, factor):
    sample, count = pl.program_id(0), pl.num_programs(0)
    rows_each = out_ref.shape[1]

    block = x_ref[0].reshape(HALF * CH, NLON)
    rows = pl.ds(pl.multiple_of(pl.program_id(1) * HALF * CH, CH), HALF * CH)
    product[rows, :] = jnp.dot(block, table_ref[...], preferred_element_type=jnp.float32)

    @pl.when(pl.program_id(1) == 1)
    def _():
        @pl.loop(0, HALF // CHUNK)
        def _(step):
            first = step * CHUNK
            for t in range(CHUNK):
                pieces = []
                for q in range(4):
                    scale = factor[...] if q < 2 else 2.0
                    for half in range(2):
                        rows = pl.ds(pl.multiple_of((half * HALF + first + t) * CH, CH), CH)
                        pieces.append(product[rows, q * LANES : (q + 1) * LANES] * scale)
                turned = jnp.concatenate(pieces, axis=0).T
                for slot in range(SLOTS):
                    row = (slot * count + sample) * HALF + first + t
                    packed[pl.ds(row, DEST, stride=rows_each), :] = turned[slot * DEST : (slot + 1) * DEST]

    @pl.when((sample == count - 1) & (pl.program_id(1) == 1))
    def _():
        for device in range(DEST):
            out_ref[device] = packed[device * rows_each : (device + 1) * rows_each, :].astype(out_ref.dtype)


def forward(pair_order, grad, start, count, table=None):
    whole = pl.BlockSpec((NLON, COLS), lambda s, half: (0, 0))
    in_specs = [
        pl.BlockSpec(memory_space=pltpu.SMEM),
        pl.BlockSpec((1, HALF, CH, NLON), lambda s, half: (s + start, half, 0, 0)),
    ]
    shape = (DEST, packed_rows(count), LANES)
    out_specs = [pl.BlockSpec(shape, lambda s, half: (0, 0, 0))]
    out_shape = [jax.ShapeDtypeStruct(shape, jnp.bfloat16)]
    scratch = [pltpu.VMEM((LAT * CH, COLS), jnp.float32), pltpu.VMEM((DEST * packed_rows(count), LANES), jnp.float32)]
    scratch.append(pltpu.VMEM((1, LANES), jnp.float32))
    if table is None:
        out_specs.append(whole)
        out_shape.append(jax.ShapeDtypeStruct((NLON, COLS), jnp.bfloat16))
        scratch += [pltpu.VMEM((96, 2 * LANES), jnp.float32)] * 2
    else:
        in_specs.append(whole)
    return pl.pallas_call(
        first_forward_kernel if table is None else later_forward_kernel,
        grid=(count, 2),
        in_specs=in_specs,
        out_specs=out_specs,
        out_shape=out_shape,
        scratch_shapes=scratch,
        compiler_params=pltpu.CompilerParams(vmem_limit_bytes=VMEM),
        cost_estimate=pl.CostEstimate(flops=4 * count * 1440 * NLON * COLS, bytes_accessed=count * 6_000_000, transcendentals=0),
        name="forward",
    )(pair_order, grad, *([] if table is None else [table]))


def place(order, pair, offset, piece, rows_each):
    return (order * GROUPS + pair * 2 + offset) * rows_each + piece * HALF


def column_tiles(count):
    return [
        (sample, pair, slice((sample * 2 + pair) * LANES, (sample * 2 + pair + 1) * LANES))
        for sample in range(count)
        for pair in range(2)
    ]


def shuffle(a, b):
    lane = lax.broadcasted_iota(jnp.int32, (HP, LANES), 1)
    former_half = lax.rem(lax.div(lane, CH), 2) == 0
    return jnp.where(former_half, a, pltpu.roll(b, CH, 1)), jnp.where(former_half, pltpu.roll(a, LANES - CH, 1), b)


def columns_kernel(count, x_ref, out_ref, wide):
    slot = pl.program_id(0)
    rows_each = x_ref.shape[1]

    @pl.when(slot == 0)
    def _():
        for device in range(DEST):
            wide[device * rows_each : (device + 1) * rows_each, :] = x_ref[device].astype(jnp.float32)
        wide[DEST * rows_each :, :] = jnp.zeros((EXTRA, LANES), jnp.float32)

    @pl.loop(0, 8)
    def _(order):
        for sample, pair, lanes in column_tiles(count):
            a, b = (wide[pl.ds(place(order, pair, offset, slot * count + sample, rows_each), HP), :] for offset in range(2))
            for half, value in enumerate(shuffle(a, b)):
                rows = pl.ds(pl.multiple_of((order * 2 + half) * HP, HP), HP)
                out_ref[0, rows, lanes] = value.astype(out_ref.dtype)


def columns_of(received, count):
    width = count * 2 * LANES
    return pl.pallas_call(
        functools.partial(columns_kernel, count),
        grid=(SLOTS,),
        in_specs=[pl.BlockSpec(received.shape, lambda slot: (0, 0, 0))],
        out_specs=pl.BlockSpec((1, 16 * HP, width), lambda slot: (slot, 0, 0)),
        out_shape=jax.ShapeDtypeStruct((SLOTS, 16 * HP, width), jnp.bfloat16),
        scratch_shapes=[pltpu.VMEM((DEST * packed_rows(count) + EXTRA, LANES), jnp.float32)],
        compiler_params=pltpu.CompilerParams(vmem_limit_bytes=VMEM),
        cost_estimate=pl.CostEstimate(flops=10_000_000, bytes_accessed=5_000_000, transcendentals=0),
        name="columns",
    )(received)


def spectral_kernel(count, low_ref, place_ref, f0, f1, columns, t0, t1, t2, t3, out_ref, legendre, split, synthesis, gains, wide, sems):
    slot = pl.program_id(0)
    group, z = place_ref[0], place_ref[1]

    rows_each = out_ref.shape[1]
    tiles = column_tiles(count)

    def table_copies(which):
        copies = []
        for other in range(GROUPS):
            for shift, source in enumerate((t0, t1, t2, t3)):
                block = other // 2 * 8 + lax.rem(z + (4 - shift), 4) * 2 + other % 2
                copies.append(pltpu.make_async_copy(source.at[other, which], legendre.at[which, block], sems.at[which, other * 4 + shift]))
        return copies

    @pl.when(slot == 0)
    def _():
        for which in range(SLOTS):
            for copy in table_copies(which):
                copy.start()
        used = SLOTS * count * HALF
        for device in range(DEST):
            wide[device * rows_each + used : (device + 1) * rows_each, :] = jnp.zeros((rows_each - used, LANES), jnp.float32)

    low = low_ref[slot]
    below = lax.broadcasted_iota(jnp.int32, (1, ROWS), 1) < M - low
    for k in range(GROUPS):
        rows = pl.ds(pl.multiple_of(jnp.bitwise_xor(group, k) * CH, CH), CH)
        for part in range(2):
            whole = (f1 if k % 2 else f0)[k // 2, part]
            gains[part, rows, :] = jnp.where(below, pltpu.roll(whole, ROWS - low, 1), pltpu.roll(whole, 1, 1))

    for copy in table_copies(slot):
        copy.wait()
    table = legendre[slot].reshape(16 * HP, ROWS)
    spectrum = lax.dot_general(columns[0], table, TN, preferred_element_type=jnp.float32)
    for sample, pair, lanes in tiles:
        a0, a1, a2, a3 = (spectrum[lanes.start + q * 32 : lanes.start + (q + 1) * 32] for q in range(4))
        former, latter = jnp.where(below, a0, a2), jnp.where(below, a1, a3)
        re = gains[0, pair * 32 : (pair + 1) * 32]
        im = gains[1, pair * 32 : (pair + 1) * 32]
        real, imag = re * former + im * latter, re * latter - im * former
        parts = (jnp.where(below, real, 0.0), jnp.where(below, imag, 0.0), jnp.where(below, 0.0, real), jnp.where(below, 0.0, imag))
        for q in range(4):
            split[lanes.start + q * 32 : lanes.start + (q + 1) * 32, :] = parts[q].astype(split.dtype)
    synthesis[...] = lax.dot_general(table, split[...], NT, preferred_element_type=jnp.float32)

    @pl.loop(0, 8)
    def _(order):
        for sample, pair, lanes in tiles:
            halves = [synthesis[pl.ds(pl.multiple_of((order * 2 + half) * HP, HP), HP), lanes] for half in range(2)]
            for offset, value in enumerate(shuffle(*halves)):
                wide[pl.ds(place(order, pair, offset, slot * count + sample, rows_each), HALF), :] = value[:HALF]

    @pl.when(slot == SLOTS - 1)
    def _():
        for device in range(DEST):
            out_ref[device] = wide[device * rows_each : (device + 1) * rows_each, :].astype(out_ref.dtype)


def spectral(low, where, filters, received, tables, count):
    width = count * 2 * LANES
    shape = (DEST, packed_rows(count), LANES)
    smem = pl.BlockSpec(memory_space=pltpu.SMEM)
    hbm = pl.BlockSpec(memory_space=pl.ANY)
    gain = pl.BlockSpec((2, 2, CH, ROWS), lambda slot: (0, 0, 0, 0))
    return pl.pallas_call(
        functools.partial(spectral_kernel, count),
        grid=(SLOTS,),
        in_specs=[smem, smem] + [gain] * 2 + [pl.BlockSpec((1, 16 * HP, width), lambda slot: (slot, 0, 0))] + [hbm] * 4,
        out_specs=pl.BlockSpec(shape, lambda slot: (0, 0, 0)),
        out_shape=jax.ShapeDtypeStruct(shape, jnp.bfloat16),
        scratch_shapes=[
            pltpu.VMEM((SLOTS, 16, HP, ROWS), jnp.bfloat16),
            pltpu.VMEM((width, ROWS), jnp.bfloat16),
            pltpu.VMEM((16 * HP, width), jnp.float32),
            pltpu.VMEM((2, GROUPS * CH, ROWS), jnp.float32),
            pltpu.VMEM((DEST * packed_rows(count) + EXTRA, LANES), jnp.float32),
            pltpu.SemaphoreType.DMA((SLOTS, 16)),
        ],
        compiler_params=pltpu.CompilerParams(vmem_limit_bytes=VMEM),
        cost_estimate=pl.CostEstimate(flops=12 * ROWS * ROWS * width, bytes_accessed=12_000_000, transcendentals=0),
        name="spectral",
    )(low, where, *filters, columns_of(received, count), *tables)


def later_inverse_kernel(scale_ref, table_ref, x_ref, done_ref, out_ref, packed, left):
    inverse_kernel(scale_ref, table_ref, x_ref, out_ref, packed, left)


def inverse_kernel(scale_ref, table_ref, x_ref, out_ref, packed, left):
    sample, count = pl.program_id(0), pl.num_programs(0)
    rows_each = x_ref.shape[1]

    @pl.when((sample == 0) & (pl.program_id(1) == 0))
    def _():
        for device in range(DEST):
            packed[device * rows_each : (device + 1) * rows_each, :] = x_ref[device].astype(jnp.float32)

    blank = jnp.zeros((LANES - PAIRS, LANES), jnp.float32)

    @pl.when(pl.program_id(1) == 0)
    def _():
        @pl.loop(0, HALF // CHUNK)
        def _(step):
            first = step * CHUNK
            for t in range(CHUNK):
                starts = [(slot * count + sample) * HALF + first + t for slot in range(SLOTS)]
                pieces = [packed[pl.ds(start, DEST, stride=rows_each), :] for start in starts]
                turned = jnp.concatenate(pieces + [blank], axis=0).T.astype(left.dtype)
                for q in range(4):
                    for half in range(2):
                        piece = turned[(q * 2 + half) * CH : (q * 2 + half + 1) * CH]
                        rows = pl.ds(pl.multiple_of((half * HALF + first + t) * CH, CH), CH)
                        left[rows, q * LANES : (q + 1) * LANES] = piece

    rows = pl.ds(pl.multiple_of(pl.program_id(1) * HALF * CH, CH), HALF * CH)
    for start in range(0, NLON, 512):
        stop = min(start + 512, NLON)
        values = lax.dot_general(left[rows, :], table_ref[start:stop, :], NT, preferred_element_type=jnp.float32)
        values = values.reshape(HALF, CH, stop - start) * scale_ref[:, :, : stop - start]
        out_ref[0, :, :, start:stop] = values.astype(out_ref.dtype)


def inverse(scale, table, received, start, count, done=None):
    in_specs = [
        pl.BlockSpec((HALF, 1, 512), lambda s, half: (half, 0, 0)),
        pl.BlockSpec((NLON, COLS), lambda s, half: (0, 0)),
        pl.BlockSpec(received.shape, lambda s, half: (0, 0, 0)),
    ]
    return pl.pallas_call(
        inverse_kernel if done is None else later_inverse_kernel,
        grid=(count, 2),
        in_specs=in_specs if done is None else in_specs + [pl.BlockSpec(memory_space=pl.ANY)],
        out_specs=pl.BlockSpec((1, HALF, CH, NLON), lambda s, half: (s + start, half, 0, 0)),
        out_shape=jax.ShapeDtypeStruct((SAMPLES, LAT, CH, NLON), jnp.bfloat16),
        input_output_aliases={} if done is None else {3: 0},
        scratch_shapes=[
            pltpu.VMEM((DEST * received.shape[1], LANES), jnp.float32),
            pltpu.VMEM((LAT * CH, COLS), jnp.bfloat16),
        ],
        compiler_params=pltpu.CompilerParams(vmem_limit_bytes=VMEM),
        cost_estimate=pl.CostEstimate(flops=4 * count * 1440 * NLON * COLS, bytes_accessed=count * 6_000_000, transcendentals=0),
        name="inverse",
    )(scale, table, received, *([] if done is None else [done]))


def padded_filters(filter_re, filter_im):
    return jnp.pad(jnp.stack([filter_re, filter_im]), ((0, 0), (0, 0), (0, ROWS - M)))


def body(grad_out, legendre, filter_re, filter_im, quad_weight, pair_order):
    group = lax.axis_index("x_hi") * 2 + lax.axis_index("core")
    z = lax.axis_index("z")
    mine = (lax.axis_index("x_lo") * 4 + lax.axis_index("y")) * GROUPS + group

    own = lax.all_to_all(legendre.reshape(GROUPS, SLOTS, HALF, ROWS), ("x_hi", "core"), 0, 0)

    far = lax.ppermute(padded_filters(filter_re, filter_im), "x_hi", [(0, 1), (1, 0)])

    grad = jnp.transpose(grad_out, (0, 2, 1, 3))
    packed, table = forward(pair_order, grad, 0, EARLY)
    packed, own, far, filter_re, filter_im = lax.optimization_barrier((packed, own, far, filter_re, filter_im))
    early = lax.all_to_all(packed, SLOT_AXES, 0, 0)
    own = jnp.pad(own, ((0, 0), (0, 0), (0, HP - HALF), (0, 0)))
    tables = [own] + [lax.ppermute(own, "z", [(i, (i + shift) % 4) for i in range(4)]) for shift in range(1, 4)]
    (packed,) = forward(pair_order, grad, EARLY, SAMPLES - EARLY, table)
    late = lax.all_to_all(packed, SLOT_AXES, 0, 0)
    near = jnp.stack([padded_filters(filter_re, filter_im), far])
    filters = [near, lax.ppermute(near, "core", [(0, 1), (1, 0)])]

    low = lax.dynamic_slice_in_dim(pair_order, mine * SLOTS, SLOTS)
    where = jnp.stack([group, z])
    early = lax.all_to_all(spectral(low, where, filters, early, tables, EARLY), SLOT_AXES, 0, 0)
    late = lax.all_to_all(spectral(low, where, filters, late, tables, SAMPLES - EARLY), SLOT_AXES, 0, 0)

    scale = jnp.broadcast_to((quad_weight * (2.0 * math.pi / NLON))[:, None, None], (LAT, 1, 512))
    values = inverse(scale, table, early, 0, EARLY)
    values = inverse(scale, table, late, EARLY, SAMPLES - EARLY, values)
    return jnp.transpose(values, (0, 2, 1, 3))


def solution(mesh):
    fine = Mesh(mesh.devices.reshape(2, 4, 2, 4, 2), ("x_lo", "y", "x_hi", "z", "core"))
    order, chan = ("x_lo", "y"), ("x_hi", "z", "core")
    in_specs = (P(None, chan, order, None), P(order, chan, None), P(chan, None), P(chan, None), P(order), P())
    return jax.shard_map(body, mesh=fine, in_specs=in_specs, out_specs=P(None, chan, order, None), check_vma=False)
```
